256 devices in a mesh: dp: 16 (over x, y_hi, core), zero: 16 (over y_lo, z).
Axes of the slice: x: 4, y: 4 (y_hi: 2, y_lo: 2; y = y_hi * 2 + y_lo), z: 8, core: 2. Of those that a mesh axis runs over, the one named last changes fastest.
Arguments:
- picture_embeds: bfloat16 [32768, 1024], P(('dp', 'zero')), may hold values from -4 to 4
- matched_slot: int32 [32768], P(('dp', 'zero')), may hold values from 0 to 2047, as said below
- summary_token_states: bfloat16 [32768, 1024], P(('dp', 'zero')), may hold values from -10 to 10
- feedforward_inner_activations: bfloat16 [32768, 4096], P(('dp', 'zero')), may hold values from -24 to 24
- closing_layernorm_multiplier: float32 [1024], replicated, may hold values from 0.1 to 1.9
- contracting_matrix: bfloat16 [4096, 1024], P('zero'), may hold values from -0.09375 to 0.09375
- sharpness_factor: float32 [1], replicated, may hold values from 3 to 6
- additive_shift_learned: float32 [1], replicated, may hold values from -3 to -1
Outputs:
- image_grad: float32 [32768, 1024], P(('dp', 'zero'))
- hidden_grad: bfloat16 [32768, 4096], P(('dp', 'zero'))
- down_grad: float32 [4096, 1024], P('zero', 'dp')
The draws below stay inside these ranges and needn't reach their ends.
Inputs may be any that keep to these rules, and one draw needn't show every extreme that they name: `matched_slot`: within the 2048 images of one zero index every position 0 to 2047 is named exactly once.
All inputs are finite; a program needn't handle non-finite values.
Results may differ from the reference program's by a relative error of at most 0.005.
Values may be sent and summed in bfloat16 or wider, within the bound.
A program may use at most 128 MiB of HBM per device.

```python
import math
import jax
import jax.numpy as jnp
from jax import lax

E = 1024
D = 1024
FF = 4096
B_DEV = 128
B_GROUP = 2048
B_TOTAL = 32768


def matched_positions(key):
    groups = B_TOTAL // B_GROUP
    cycle_count = B_GROUP // B_DEV
    group_keys = jax.random.split(jax.random.fold_in(key, 37), groups)
    orders = jax.vmap(lambda one_key: jax.random.permutation(one_key, B_GROUP))(group_keys)
    return orders.reshape(groups, cycle_count, B_DEV).swapaxes(0, 1).reshape(B_TOTAL).astype(jnp.int32)


def paired_fields(key):
    groups = B_TOTAL // B_GROUP
    keys = jax.random.split(jax.random.fold_in(key, 53), 9)
    cluster_ids = jax.random.randint(keys[0], (B_TOTAL,), 0, 32)
    amplitude = jax.random.uniform(keys[1], (32, 1), minval=0.5, maxval=1.5)
    centres = jax.random.normal(keys[2], (32, E))
    latent_noise = jax.random.normal(keys[3], (B_TOTAL, E))
    image_noise = jax.random.normal(keys[4], (B_TOTAL, E))
    caption_noise = jax.random.normal(keys[5], (B_TOTAL, E))
    latent = (centres * amplitude)[cluster_ids] + latent_noise
    image_base = jnp.clip((latent + image_noise) / 1.8, -4.0, 4.0)
    positions = matched_positions(key)
    rows = jnp.arange(B_TOTAL, dtype=jnp.int32)
    group_of = rows // B_DEV % groups
    target = (positions // B_DEV * groups + group_of) * B_DEV + positions % B_DEV
    caption_latent = jnp.zeros((B_TOTAL, E), jnp.float32).at[target].set(latent)
    caption_base = jnp.clip((caption_latent + caption_noise) / 1.8, -4.0, 4.0)
    image_scale = jnp.exp(jax.random.uniform(keys[7], (B_TOTAL, 1), minval=math.log(0.1), maxval=math.log(1.0)))
    caption_scale = jnp.exp(jax.random.uniform(keys[8], (B_TOTAL, 1), minval=math.log(0.25), maxval=math.log(2.5)))
    return (image_base * image_scale, caption_base * caption_scale)


def draw_picture_embeds(key, part):
    return paired_fields(key)[0].astype(jnp.bfloat16)


def draw_summary_token_states(key, part):
    return paired_fields(key)[1].astype(jnp.bfloat16)


def draw_matched_slot(key, part):
    return matched_positions(key)


def with_spikes(entries, own_key, source, target, parts, factor):
    def block_of(position):
        return (jnp.arange(entries.shape[position]) // (entries.shape[position] // parts)).reshape((-1,) + (1,) * (entries.ndim - 1 - position))

    one_side = jax.random.permutation(own_key, parts)[block_of(target)]
    far = (block_of(target) + parts // 2) % parts
    return jnp.where((block_of(source) == one_side) | (block_of(source) == far), factor * entries, entries)


def block_levels(own_key, shape, pieces, low, largest):
    gain, own = 1.0, jax.random.fold_in(own_key, 6)
    for position, blocks in pieces:
        draws = jnp.exp(jax.random.uniform(jax.random.fold_in(own, position), (blocks,), jnp.float32, low / len(pieces), largest / len(pieces)))
        gain = gain * jnp.repeat(draws, shape[position] // blocks).reshape([-1 if axis == position else 1 for axis in range(len(shape))])
    return gain


def normal_values(own_key, shape, scale, bound, cuts=(), held_as=jnp.bfloat16):
    gain = block_levels(own_key, shape, cuts, -0.22, 0.18) if cuts else 1.0
    result = jax.random.normal(own_key, shape, jnp.float32) * scale * gain
    return jnp.minimum(jnp.maximum(result, -bound), bound).astype(held_as)


def heavy_noise(rng, dims, deviation, bound, cuts, heavy, held_as=jnp.bfloat16):
    entries = deviation * jax.random.normal(rng, dims, jnp.float32)
    if cuts:
        entries = entries * block_levels(rng, dims, cuts, -0.22, 0.18)
    return jnp.clip(with_spikes(entries, jax.random.fold_in(rng, 3), *heavy), -bound, bound).astype(held_as)


def setup_inputs(seed: int = 0) -> dict:
    arg_keys = jax.random.split(jax.random.key(seed), 9)
    picture_embeds = draw_picture_embeds(jax.random.fold_in(arg_keys[8], 71), 0)
    matched_slot = draw_matched_slot(jax.random.fold_in(arg_keys[8], 71), 0)
    summary_token_states = draw_summary_token_states(jax.random.fold_in(arg_keys[8], 71), 0)
    feedforward_inner_activations = heavy_noise(arg_keys[3], (B_TOTAL, FF), 1.0, 24.0, ((0, 256),), (0, 1, 256, 6.0))
    closing_layernorm_multiplier = jnp.clip(1.0 + 0.18 * jax.random.normal(arg_keys[4], (D,), jnp.float32), 0.1, 1.9)
    contracting_matrix = normal_values(arg_keys[5], (FF, D), FF ** -0.5, 0.09375, ((0, 16),))
    sharpness_factor = jnp.clip(jax.random.uniform(arg_keys[6], (1,), jnp.float32, 3.0, 6.0), 3.0, 6.0)
    additive_shift_learned = jnp.clip(jax.random.uniform(arg_keys[7], (1,), jnp.float32, -3.0, -1.0), -3.0, -1.0)
    return dict(picture_embeds=picture_embeds, matched_slot=matched_slot, summary_token_states=summary_token_states, feedforward_inner_activations=feedforward_inner_activations, closing_layernorm_multiplier=closing_layernorm_multiplier, contracting_matrix=contracting_matrix, sharpness_factor=sharpness_factor, additive_shift_learned=additive_shift_learned)


def unit_rows(values):
    return values * lax.rsqrt(lax.optimization_barrier(jnp.sum(values * values, axis=1, keepdims=True)) + 1e-06)

def text_embed(features, closing_layernorm_multiplier):
    center = features - lax.optimization_barrier(jnp.mean(features, axis=1, keepdims=True))
    spread = lax.optimization_barrier(jnp.mean(center * center, axis=1, keepdims=True))
    return unit_rows(center * lax.rsqrt(spread + 1e-05) * closing_layernorm_multiplier)

def pair_terms(image_b, matched_slot, caption_b, start, similarity_multiplier, shift_value):
    scores = similarity_multiplier * lax.dot_general(image_b, caption_b, (((1,), (1,)), ((), ())), preferred_element_type=jnp.float32) + shift_value
    places = start + jnp.arange(caption_b.shape[0], dtype=jnp.int32)
    labels = jnp.where(matched_slot[:, None] == places[None, :], 1.0, -1.0).astype(scores.dtype)
    weights = (-labels * jax.nn.sigmoid(-labels * scores)).astype(jnp.bfloat16)
    image_term = similarity_multiplier * jnp.dot(weights, caption_b, preferred_element_type=jnp.float32)
    caption_term = similarity_multiplier * lax.dot_general(weights, image_b, (((0,), (0,)), ((), ())), preferred_element_type=jnp.float32)
    return (image_term, caption_term)

def reference(picture_embeds, matched_slot, summary_token_states, feedforward_inner_activations, closing_layernorm_multiplier, contracting_matrix, sharpness_factor, additive_shift_learned):
    groups = B_TOTAL // B_GROUP
    cycle_count = B_GROUP // B_DEV
    similarity_multiplier = sharpness_factor[0]
    shift_value = additive_shift_learned[0]
    unit_image, image_back = jax.vjp(unit_rows, picture_embeds.astype(jnp.float32))
    image_b = unit_image.astype(jnp.bfloat16)
    caption, caption_back = jax.vjp(lambda feats: text_embed(feats, closing_layernorm_multiplier), summary_token_states.astype(jnp.float32))
    caption_b = caption.astype(jnp.bfloat16)

    def regroup(values):
        rest = values.shape[1:]
        return values.reshape((cycle_count, groups, B_DEV) + rest).swapaxes(0, 1).reshape((groups, B_GROUP) + rest)

    def ungroup(values):
        rest = values.shape[2:]
        return values.reshape((groups, cycle_count, B_DEV) + rest).swapaxes(0, 1).reshape((B_TOTAL,) + rest)

    def one_group(items):
        image_group, partner_group, caption_group = items
        return pair_terms(image_group, partner_group, caption_group, jnp.int32(0), similarity_multiplier, shift_value)
    image_terms, caption_terms = lax.map(one_group, (regroup(image_b), regroup(matched_slot), regroup(caption_b)))
    image_grad = image_back(ungroup(image_terms))[0]
    upstream = caption_back(ungroup(caption_terms))[0].astype(jnp.bfloat16)
    hidden_grad = lax.dot_general(upstream, contracting_matrix, (((1,), (1,)), ((), ())), preferred_element_type=jnp.float32).astype(jnp.bfloat16)
    down_grad = lax.dot_general(feedforward_inner_activations, upstream, (((0,), (0,)), ((), ())), preferred_element_type=jnp.float32)
    return (image_grad, hidden_grad, down_grad)
```

```python
import jax
import jax.numpy as jnp
from jax import lax
from jax.sharding import PartitionSpec as P


def unit_rows(values):
    return values * lax.rsqrt(jnp.sum(values * values, axis=1, keepdims=True) + 1e-06)


def text_embed(features, closing_layernorm_multiplier):
    center = features - jnp.mean(features, axis=1, keepdims=True)
    spread = jnp.mean(center * center, axis=1, keepdims=True)
    return unit_rows(center * lax.rsqrt(spread + 1e-05) * closing_layernorm_multiplier)


def sigmoid_weights(scores, labels):
    return (-labels * jax.nn.sigmoid(-labels * scores)).astype(jnp.bfloat16)


def shards(
    picture_embeds,
    matched_slot,
    summary_token_states,
    feedforward_inner_activations,
    closing_layernorm_multiplier,
    contracting_matrix,
    sharpness_factor,
    additive_shift_learned,
):
    similarity_multiplier = sharpness_factor[0]
    shift_value = additive_shift_learned[0]
    local_rows, width = picture_embeds.shape
    own_start = lax.axis_index("dp") * local_rows

    ffa_cols = lax.all_to_all(
        feedforward_inner_activations, "zero", split_axis=1, concat_axis=0, tiled=True
    )

    both = jnp.concatenate([picture_embeds, summary_token_states], axis=1)
    both_g = lax.all_gather(both, "dp", axis=0, tiled=True)
    slot_g = lax.all_gather(matched_slot, "dp", axis=0, tiled=True)
    image_b_g = unit_rows(both_g[:, :width].astype(jnp.float32)).astype(jnp.bfloat16)
    caption_b_g = text_embed(
        both_g[:, width:].astype(jnp.float32), closing_layernorm_multiplier
    ).astype(jnp.bfloat16)

    unit_image, image_back = jax.vjp(unit_rows, picture_embeds.astype(jnp.float32))
    image_b = unit_image.astype(jnp.bfloat16)
    caption, caption_back = jax.vjp(
        lambda feats: text_embed(feats, closing_layernorm_multiplier),
        summary_token_states.astype(jnp.float32),
    )
    caption_b = caption.astype(jnp.bfloat16)
    group_rows = caption_b_g.shape[0]

    scores_i = (
        similarity_multiplier
        * lax.dot_general(
            image_b, caption_b_g, (((1,), (1,)), ((), ())), preferred_element_type=jnp.float32
        )
        + shift_value
    )
    places = jnp.arange(group_rows, dtype=jnp.int32)
    labels_i = jnp.where(matched_slot[:, None] == places[None, :], 1.0, -1.0)
    weights_i = sigmoid_weights(scores_i, labels_i)
    image_term = similarity_multiplier * jnp.dot(
        weights_i, caption_b_g, preferred_element_type=jnp.float32
    )

    scores_c = (
        similarity_multiplier
        * lax.dot_general(
            image_b_g, caption_b, (((1,), (1,)), ((), ())), preferred_element_type=jnp.float32
        )
        + shift_value
    )
    own_places = own_start + jnp.arange(local_rows, dtype=jnp.int32)
    labels_c = jnp.where(slot_g[:, None] == own_places[None, :], 1.0, -1.0)
    weights_c = sigmoid_weights(scores_c, labels_c)
    caption_term = similarity_multiplier * lax.dot_general(
        weights_c, image_b_g, (((0,), (0,)), ((), ())), preferred_element_type=jnp.float32
    )

    image_grad = image_back(image_term)[0]
    upstream = caption_back(caption_term)[0].astype(jnp.bfloat16)

    upstream_g = lax.all_gather(upstream, "zero", axis=0, tiled=True)
    hidden_part = lax.dot_general(
        upstream_g,
        contracting_matrix,
        (((1,), (1,)), ((), ())),
        preferred_element_type=jnp.float32,
    ).astype(jnp.bfloat16)
    hidden_grad = lax.all_to_all(hidden_part, "zero", split_axis=0, concat_axis=1, tiled=True)
    zero_sum = lax.dot_general(
        ffa_cols, upstream_g, (((0,), (0,)), ((), ())), preferred_element_type=jnp.float32
    )
    down_grad = lax.psum_scatter(zero_sum, "dp", scatter_dimension=1, tiled=True)
    return (image_grad, hidden_grad, down_grad)


def solution(mesh):
    placed = (
        P(("dp", "zero"), None),
        P(("dp", "zero")),
        P(("dp", "zero"), None),
        P(("dp", "zero"), None),
        P(),
        P("zero", None),
        P(),
        P(),
    )
    return jax.shard_map(
        shards,
        mesh=mesh,
        in_specs=placed,
        out_specs=(P(("dp", "zero"), None), P(("dp", "zero"), None), P("zero", "dp")),
        check_vma=False,
    )
```

```python
import jax
import jax.numpy as jnp
from jax import lax
from jax.sharding import PartitionSpec as P


def unit_rows(values):
    return values * lax.rsqrt(jnp.sum(values * values, axis=1, keepdims=True) + 1e-06)


def text_embed(features, closing_layernorm_multiplier):
    center = features - jnp.mean(features, axis=1, keepdims=True)
    spread = jnp.mean(center * center, axis=1, keepdims=True)
    return unit_rows(center * lax.rsqrt(spread + 1e-05) * closing_layernorm_multiplier)


def sigmoid_weights(scores, labels):
    return (-labels * jax.nn.sigmoid(-labels * scores)).astype(jnp.bfloat16)


def shards(
    picture_embeds,
    matched_slot,
    summary_token_states,
    feedforward_inner_activations,
    closing_layernorm_multiplier,
    contracting_matrix,
    sharpness_factor,
    additive_shift_learned,
):
    similarity_multiplier = sharpness_factor[0]
    shift_value = additive_shift_learned[0]
    local_rows, width = picture_embeds.shape
    own_start = lax.axis_index("dp") * local_rows

    ffa_cols = lax.all_to_all(
        feedforward_inner_activations, "zero", split_axis=1, concat_axis=0, tiled=True
    )

    digits = jnp.zeros((local_rows, 128), jnp.bfloat16)
    digits = digits.at[:, 0].set((matched_slot // 256).astype(jnp.bfloat16))
    digits = digits.at[:, 1].set((matched_slot % 256).astype(jnp.bfloat16))
    both = jnp.concatenate([picture_embeds, summary_token_states, digits], axis=1)
    both_g = lax.all_gather(both, "dp", axis=0, tiled=True)
    ffa_cols, both_g = lax.optimization_barrier((ffa_cols, both_g))
    slot_g = both_g[:, 2 * width].astype(jnp.int32) * 256 + both_g[:, 2 * width + 1].astype(
        jnp.int32
    )
    image_b_g = unit_rows(both_g[:, :width].astype(jnp.float32)).astype(jnp.bfloat16)
    caption_b_g = text_embed(
        both_g[:, width : 2 * width].astype(jnp.float32), closing_layernorm_multiplier
    ).astype(jnp.bfloat16)

    unit_image, image_back = jax.vjp(unit_rows, picture_embeds.astype(jnp.float32))
    image_b = unit_image.astype(jnp.bfloat16)
    caption, caption_back = jax.vjp(
        lambda feats: text_embed(feats, closing_layernorm_multiplier),
        summary_token_states.astype(jnp.float32),
    )
    caption_b = caption.astype(jnp.bfloat16)
    group_rows = caption_b_g.shape[0]

    scores_i = (
        similarity_multiplier
        * lax.dot_general(
            image_b, caption_b_g, (((1,), (1,)), ((), ())), preferred_element_type=jnp.float32
        )
        + shift_value
    )
    places = jnp.arange(group_rows, dtype=jnp.int32)
    labels_i = jnp.where(matched_slot[:, None] == places[None, :], 1.0, -1.0)
    weights_i = sigmoid_weights(scores_i, labels_i)
    image_term = similarity_multiplier * jnp.dot(
        weights_i, caption_b_g, preferred_element_type=jnp.float32
    )

    scores_c = (
        similarity_multiplier
        * lax.dot_general(
            image_b_g, caption_b, (((1,), (1,)), ((), ())), preferred_element_type=jnp.float32
        )
        + shift_value
    )
    own_places = own_start + jnp.arange(local_rows, dtype=jnp.int32)
    labels_c = jnp.where(slot_g[:, None] == own_places[None, :], 1.0, -1.0)
    weights_c = sigmoid_weights(scores_c, labels_c)
    caption_term = similarity_multiplier * lax.dot_general(
        weights_c, image_b_g, (((0,), (0,)), ((), ())), preferred_element_type=jnp.float32
    )

    image_grad = image_back(image_term)[0]
    upstream = caption_back(caption_term)[0].astype(jnp.bfloat16)

    zero_size = lax.axis_size("zero")
    upstream_rep = jnp.broadcast_to(upstream[None], (zero_size,) + upstream.shape)
    upstream_g = lax.all_to_all(
        upstream_rep.reshape((zero_size * local_rows, width)),
        "zero",
        split_axis=0,
        concat_axis=0,
        tiled=True,
    )
    hidden_part = lax.dot_general(
        upstream_g,
        contracting_matrix,
        (((1,), (1,)), ((), ())),
        preferred_element_type=jnp.float32,
    ).astype(jnp.bfloat16)
    hidden_grad = lax.all_to_all(hidden_part, "zero", split_axis=0, concat_axis=1, tiled=True)
    zero_sum = lax.dot_general(
        ffa_cols, upstream_g, (((0,), (0,)), ((), ())), preferred_element_type=jnp.float32
    )
    dp_size = lax.axis_size("dp")
    down_parts = lax.all_to_all(zero_sum, "dp", split_axis=1, concat_axis=0, tiled=True)
    down_grad = jnp.sum(down_parts.reshape((dp_size,) + (zero_sum.shape[0], -1)), axis=0)
    return (image_grad, hidden_grad, down_grad)


def solution(mesh):
    placed = (
        P(("dp", "zero"), None),
        P(("dp", "zero")),
        P(("dp", "zero"), None),
        P(("dp", "zero"), None),
        P(),
        P("zero", None),
        P(),
        P(),
    )
    return jax.shard_map(
        shards,
        mesh=mesh,
        in_specs=placed,
        out_specs=(P(("dp", "zero"), None), P(("dp", "zero"), None), P("zero", "dp")),
        check_vma=False,
    )
```

```python
import jax
import jax.numpy as jnp
from jax import lax
from jax.sharding import PartitionSpec as P


def unit_rows(values):
    return values * lax.rsqrt(jnp.sum(values * values, axis=1, keepdims=True) + 1e-06)


def text_embed(features, closing_layernorm_multiplier):
    center = features - jnp.mean(features, axis=1, keepdims=True)
    spread = jnp.mean(center * center, axis=1, keepdims=True)
    return unit_rows(center * lax.rsqrt(spread + 1e-05) * closing_layernorm_multiplier)


def sigmoid_weights(scores, labels):
    return (-labels * jax.nn.sigmoid(-labels * scores)).astype(jnp.bfloat16)


def shards(
    picture_embeds,
    matched_slot,
    summary_token_states,
    feedforward_inner_activations,
    closing_layernorm_multiplier,
    contracting_matrix,
    sharpness_factor,
    additive_shift_learned,
):
    similarity_multiplier = sharpness_factor[0]
    shift_value = additive_shift_learned[0]
    local_rows, width = picture_embeds.shape

    dp_size = lax.axis_size("dp")
    zero_size = lax.axis_size("zero")
    dp_place = lax.axis_index("dp")
    own_start = dp_place * local_rows
    transpose_route = [
        (a * zero_size + b, b * zero_size + a) for a in range(dp_size) for b in range(zero_size)
    ]

    ffa_cols = lax.all_to_all(
        feedforward_inner_activations, "dp", split_axis=1, concat_axis=0, tiled=True
    )
    weight_block = lax.ppermute(contracting_matrix, ("dp", "zero"), transpose_route)

    digits = jnp.zeros((local_rows, 128), jnp.bfloat16)
    digits = digits.at[:, 0].set((matched_slot // 256).astype(jnp.bfloat16))
    digits = digits.at[:, 1].set((matched_slot % 256).astype(jnp.bfloat16))
    both = jnp.concatenate([picture_embeds, summary_token_states, digits], axis=1)
    both_g = lax.all_gather(both, "dp", axis=0, tiled=True)
    ffa_cols, weight_block, both_g = lax.optimization_barrier((ffa_cols, weight_block, both_g))
    slot_g = both_g[:, 2 * width].astype(jnp.int32) * 256 + both_g[:, 2 * width + 1].astype(
        jnp.int32
    )
    image_b_g = unit_rows(both_g[:, :width].astype(jnp.float32)).astype(jnp.bfloat16)
    caption_g, caption_back = jax.vjp(
        lambda feats: text_embed(feats, closing_layernorm_multiplier),
        both_g[:, width : 2 * width].astype(jnp.float32),
    )
    caption_b_g = caption_g.astype(jnp.bfloat16)
    group_rows = caption_b_g.shape[0]

    unit_image, image_back = jax.vjp(unit_rows, picture_embeds.astype(jnp.float32))

    scores = (
        similarity_multiplier
        * lax.dot_general(
            image_b_g, caption_b_g, (((1,), (1,)), ((), ())), preferred_element_type=jnp.float32
        )
        + shift_value
    )
    places = jnp.arange(group_rows, dtype=jnp.int32)
    labels = jnp.where(slot_g[:, None] == places[None, :], 1.0, -1.0)
    weights = sigmoid_weights(scores, labels)
    own_weights = lax.dynamic_slice_in_dim(weights, own_start, local_rows, axis=0)
    image_term = similarity_multiplier * jnp.dot(
        own_weights, caption_b_g, preferred_element_type=jnp.float32
    )
    caption_term = similarity_multiplier * lax.dot_general(
        weights, image_b_g, (((0,), (0,)), ((), ())), preferred_element_type=jnp.float32
    )

    image_grad = image_back(image_term)[0]
    upstream_g = caption_back(caption_term)[0].astype(jnp.bfloat16)

    hidden_part = lax.dot_general(
        upstream_g,
        weight_block,
        (((1,), (1,)), ((), ())),
        preferred_element_type=jnp.float32,
    ).astype(jnp.bfloat16)
    hidden_grad = lax.all_to_all(hidden_part, "dp", split_axis=0, concat_axis=1, tiled=True)
    group_sum = lax.dot_general(
        ffa_cols, upstream_g, (((0,), (0,)), ((), ())), preferred_element_type=jnp.float32
    )
    down_parts = lax.all_to_all(group_sum, "zero", split_axis=1, concat_axis=0, tiled=True)
    down_block = jnp.sum(down_parts.reshape((zero_size,) + (group_sum.shape[0], -1)), axis=0)
    down_grad = lax.ppermute(down_block, ("dp", "zero"), transpose_route)
    return (image_grad, hidden_grad, down_grad)


def solution(mesh):
    placed = (
        P(("dp", "zero"), None),
        P(("dp", "zero")),
        P(("dp", "zero"), None),
        P(("dp", "zero"), None),
        P(),
        P("zero", None),
        P(),
        P(),
    )
    return jax.shard_map(
        shards,
        mesh=mesh,
        in_specs=placed,
        out_specs=(P(("dp", "zero"), None), P(("dp", "zero"), None), P("zero", "dp")),
        check_vma=False,
    )
```

```python
import jax
import jax.numpy as jnp
from jax import lax
from jax.sharding import PartitionSpec as P


def unit_rows(values):
    return values * lax.rsqrt(jnp.sum(values * values, axis=1, keepdims=True) + 1e-06)


def text_embed(features, closing_layernorm_multiplier):
    center = features - jnp.mean(features, axis=1, keepdims=True)
    spread = jnp.mean(center * center, axis=1, keepdims=True)
    return unit_rows(center * lax.rsqrt(spread + 1e-05) * closing_layernorm_multiplier)


def sigmoid_weights(scores, labels):
    return (-labels * jax.nn.sigmoid(-labels * scores)).astype(jnp.bfloat16)


def shards(
    picture_embeds,
    matched_slot,
    summary_token_states,
    feedforward_inner_activations,
    closing_layernorm_multiplier,
    contracting_matrix,
    sharpness_factor,
    additive_shift_learned,
):
    similarity_multiplier = sharpness_factor[0]
    shift_value = additive_shift_learned[0]
    local_rows, width = picture_embeds.shape

    dp_size = lax.axis_size("dp")
    zero_size = lax.axis_size("zero")
    dp_place = lax.axis_index("dp")
    own_start = dp_place * local_rows
    transpose_route = [
        (a * zero_size + b, b * zero_size + a) for a in range(dp_size) for b in range(zero_size)
    ]

    digits = jnp.zeros((local_rows, 128), jnp.bfloat16)
    digits = digits.at[:, 0].set((matched_slot // 256).astype(jnp.bfloat16))
    digits = digits.at[:, 1].set((matched_slot % 256).astype(jnp.bfloat16))
    both = jnp.concatenate([picture_embeds, summary_token_states, digits], axis=1)
    both_g = lax.all_gather(both, "dp", axis=0, tiled=True)

    ffa_in, weight_in, both_g = lax.optimization_barrier(
        (feedforward_inner_activations, contracting_matrix, both_g)
    )
    ffa_cols = lax.all_to_all(ffa_in, "dp", split_axis=1, concat_axis=0, tiled=True)
    weight_block = lax.ppermute(weight_in, ("dp", "zero"), transpose_route)
    slot_g = both_g[:, 2 * width].astype(jnp.int32) * 256 + both_g[:, 2 * width + 1].astype(
        jnp.int32
    )
    image_b_g = unit_rows(both_g[:, :width].astype(jnp.float32)).astype(jnp.bfloat16)
    caption_g, caption_back = jax.vjp(
        lambda feats: text_embed(feats, closing_layernorm_multiplier),
        both_g[:, width : 2 * width].astype(jnp.float32),
    )
    caption_b_g = caption_g.astype(jnp.bfloat16)
    group_rows = caption_b_g.shape[0]

    unit_image, image_back = jax.vjp(unit_rows, picture_embeds.astype(jnp.float32))

    scores = (
        similarity_multiplier
        * lax.dot_general(
            image_b_g, caption_b_g, (((1,), (1,)), ((), ())), preferred_element_type=jnp.float32
        )
        + shift_value
    )
    places = jnp.arange(group_rows, dtype=jnp.int32)
    labels = jnp.where(slot_g[:, None] == places[None, :], 1.0, -1.0)
    weights = sigmoid_weights(scores, labels)
    own_weights = lax.dynamic_slice_in_dim(weights, own_start, local_rows, axis=0)
    image_term = similarity_multiplier * jnp.dot(
        own_weights, caption_b_g, preferred_element_type=jnp.float32
    )
    caption_term = similarity_multiplier * lax.dot_general(
        weights, image_b_g, (((0,), (0,)), ((), ())), preferred_element_type=jnp.float32
    )

    image_grad = image_back(image_term)[0]
    upstream_g = caption_back(caption_term)[0].astype(jnp.bfloat16)

    hidden_part = lax.dot_general(
        upstream_g,
        weight_block,
        (((1,), (1,)), ((), ())),
        preferred_element_type=jnp.float32,
    ).astype(jnp.bfloat16)
    hidden_grad = lax.all_to_all(hidden_part, "dp", split_axis=0, concat_axis=1, tiled=True)
    group_sum = lax.dot_general(
        ffa_cols, upstream_g, (((0,), (0,)), ((), ())), preferred_element_type=jnp.float32
    )
    down_parts = lax.all_to_all(group_sum, "zero", split_axis=1, concat_axis=0, tiled=True)
    down_block = jnp.sum(down_parts.reshape((zero_size,) + (group_sum.shape[0], -1)), axis=0)
    down_grad = lax.ppermute(down_block, ("dp", "zero"), transpose_route)
    return (image_grad, hidden_grad, down_grad)


def solution(mesh):
    placed = (
        P(("dp", "zero"), None),
        P(("dp", "zero")),
        P(("dp", "zero"), None),
        P(("dp", "zero"), None),
        P(),
        P("zero", None),
        P(),
        P(),
    )
    return jax.shard_map(
        shards,
        mesh=mesh,
        in_specs=placed,
        out_specs=(P(("dp", "zero"), None), P(("dp", "zero"), None), P("zero", "dp")),
        check_vma=False,
    )
```

```python
import functools

import jax
import jax.numpy as jnp
from jax import lax
from jax.experimental import pallas as pl
from jax.experimental.pallas import tpu as pltpu
from jax.sharding import PartitionSpec as P

MESH = pl.DeviceIdType.MESH


def gather_kernel(chips, block_ref, out_ref, send_sem, recv_sem, local_sem):
    me = lax.axis_index("dp")
    zz = lax.axis_index("zero")
    core = me % 2
    chip = me // 2
    sibling = me + 1 - 2 * core

    def peer(k):
        return ((chip + k) % chips) * 2 + core

    def source(k):
        return ((chip + chips - k) % chips) * 2 + core

    barrier = pltpu.get_barrier_semaphore()
    pl.semaphore_signal(barrier, inc=1, device_id=(sibling, zz), device_id_type=MESH)
    for k in range(1, chips):
        pl.semaphore_signal(barrier, inc=1, device_id=(peer(k), zz), device_id_type=MESH)
    pl.semaphore_wait(barrier, chips)

    local = pltpu.make_async_copy(block_ref, out_ref.at[me], local_sem)
    local.start()
    sends = []
    for k in range(1, chips):
        copy = pltpu.make_async_remote_copy(
            src_ref=block_ref,
            dst_ref=out_ref.at[me],
            send_sem=send_sem.at[k],
            recv_sem=recv_sem.at[me],
            device_id=(peer(k), zz),
            device_id_type=MESH,
        )
        copy.start()
        sends.append(copy)
    copy = pltpu.make_async_remote_copy(
        src_ref=block_ref,
        dst_ref=out_ref.at[me],
        send_sem=send_sem.at[0],
        recv_sem=recv_sem.at[me],
        device_id=(sibling, zz),
        device_id_type=MESH,
    )
    copy.start()
    sends.append(copy)
    for k in range(1, chips):
        s = source(k)
        arrived = pltpu.make_async_remote_copy(
            src_ref=out_ref.at[s],
            dst_ref=out_ref.at[s],
            send_sem=send_sem.at[chips + k],
            recv_sem=recv_sem.at[s],
            device_id=(sibling, zz),
            device_id_type=MESH,
        )
        arrived.wait_recv()
        arrived.start()
        sends.append(arrived)
    for k in range(chips):
        t = ((chip + k) % chips) * 2 + (1 - core)
        pltpu.make_async_remote_copy(
            src_ref=out_ref.at[t],
            dst_ref=out_ref.at[t],
            send_sem=send_sem.at[0],
            recv_sem=recv_sem.at[t],
            device_id=(sibling, zz),
            device_id_type=MESH,
        ).wait_recv()
    for copy in sends:
        copy.wait_send()
    local.wait()


def gather_dp(block):
    dp_size = lax.axis_size("dp")
    return pl.pallas_call(
        functools.partial(gather_kernel, dp_size // 2),
        out_shape=jax.ShapeDtypeStruct((dp_size,) + block.shape, block.dtype),
        in_specs=[pl.BlockSpec(memory_space=pl.ANY)],
        out_specs=pl.BlockSpec(memory_space=pl.ANY),
        scratch_shapes=[
            pltpu.SemaphoreType.DMA((dp_size,)),
            pltpu.SemaphoreType.DMA((dp_size,)),
            pltpu.SemaphoreType.DMA(()),
        ],
        compiler_params=pltpu.CompilerParams(collective_id=0, has_side_effects=True),
    )(block)


def unit_rows(values):
    return values * lax.rsqrt(jnp.sum(values * values, axis=1, keepdims=True) + 1e-06)


def text_embed(features, closing_layernorm_multiplier):
    center = features - jnp.mean(features, axis=1, keepdims=True)
    spread = jnp.mean(center * center, axis=1, keepdims=True)
    return unit_rows(center * lax.rsqrt(spread + 1e-05) * closing_layernorm_multiplier)


def sigmoid_weights(scores, labels):
    return (-labels * jax.nn.sigmoid(-labels * scores)).astype(jnp.bfloat16)


def shards(
    picture_embeds,
    matched_slot,
    summary_token_states,
    feedforward_inner_activations,
    closing_layernorm_multiplier,
    contracting_matrix,
    sharpness_factor,
    additive_shift_learned,
):
    similarity_multiplier = sharpness_factor[0]
    shift_value = additive_shift_learned[0]
    local_rows, width = picture_embeds.shape

    dp_size = lax.axis_size("dp")
    zero_size = lax.axis_size("zero")
    dp_place = lax.axis_index("dp")
    own_start = dp_place * local_rows
    transpose_route = [
        (a * zero_size + b, b * zero_size + a) for a in range(dp_size) for b in range(zero_size)
    ]

    ffa_cols = lax.all_to_all(
        feedforward_inner_activations, "dp", split_axis=1, concat_axis=0, tiled=True
    )
    weight_block = lax.ppermute(contracting_matrix, ("dp", "zero"), transpose_route)

    digits = jnp.zeros((local_rows, 128), jnp.bfloat16)
    digits = digits.at[:, 0].set((matched_slot // 256).astype(jnp.bfloat16))
    digits = digits.at[:, 1].set((matched_slot % 256).astype(jnp.bfloat16))
    both = jnp.concatenate([picture_embeds, summary_token_states, digits], axis=1)
    both_g = gather_dp(both).reshape((-1, both.shape[1]))
    ffa_cols, weight_block, both_g = lax.optimization_barrier((ffa_cols, weight_block, both_g))
    slot_g = both_g[:, 2 * width].astype(jnp.int32) * 256 + both_g[:, 2 * width + 1].astype(
        jnp.int32
    )
    image_b_g = unit_rows(both_g[:, :width].astype(jnp.float32)).astype(jnp.bfloat16)
    caption_g, caption_back = jax.vjp(
        lambda feats: text_embed(feats, closing_layernorm_multiplier),
        both_g[:, width : 2 * width].astype(jnp.float32),
    )
    caption_b_g = caption_g.astype(jnp.bfloat16)
    group_rows = caption_b_g.shape[0]

    unit_image, image_back = jax.vjp(unit_rows, picture_embeds.astype(jnp.float32))

    scores = (
        similarity_multiplier
        * lax.dot_general(
            image_b_g, caption_b_g, (((1,), (1,)), ((), ())), preferred_element_type=jnp.float32
        )
        + shift_value
    )
    places = jnp.arange(group_rows, dtype=jnp.int32)
    labels = jnp.where(slot_g[:, None] == places[None, :], 1.0, -1.0)
    weights = sigmoid_weights(scores, labels)
    own_weights = lax.dynamic_slice_in_dim(weights, own_start, local_rows, axis=0)
    image_term = similarity_multiplier * jnp.dot(
        own_weights, caption_b_g, preferred_element_type=jnp.float32
    )
    caption_term = similarity_multiplier * lax.dot_general(
        weights, image_b_g, (((0,), (0,)), ((), ())), preferred_element_type=jnp.float32
    )

    image_grad = image_back(image_term)[0]
    upstream_g = caption_back(caption_term)[0].astype(jnp.bfloat16)

    hidden_part = lax.dot_general(
        upstream_g,
        weight_block,
        (((1,), (1,)), ((), ())),
        preferred_element_type=jnp.float32,
    ).astype(jnp.bfloat16)
    hidden_grad = lax.all_to_all(hidden_part, "dp", split_axis=0, concat_axis=1, tiled=True)
    group_sum = lax.dot_general(
        ffa_cols, upstream_g, (((0,), (0,)), ((), ())), preferred_element_type=jnp.float32
    )
    down_parts = lax.all_to_all(group_sum, "zero", split_axis=1, concat_axis=0, tiled=True)
    down_block = jnp.sum(down_parts.reshape((zero_size,) + (group_sum.shape[0], -1)), axis=0)
    down_grad = lax.ppermute(down_block, ("dp", "zero"), transpose_route)
    return (image_grad, hidden_grad, down_grad)


def solution(mesh):
    placed = (
        P(("dp", "zero"), None),
        P(("dp", "zero")),
        P(("dp", "zero"), None),
        P(("dp", "zero"), None),
        P(),
        P("zero", None),
        P(),
        P(),
    )
    return jax.shard_map(
        shards,
        mesh=mesh,
        in_specs=placed,
        out_specs=(P(("dp", "zero"), None), P(("dp", "zero"), None), P("zero", "dp")),
        check_vma=False,
    )
```

```python
import functools

import jax
import jax.numpy as jnp
from jax import lax
from jax.experimental import pallas as pl
from jax.experimental.pallas import tpu as pltpu
from jax.sharding import PartitionSpec as P

MESH = pl.DeviceIdType.MESH


def gather_kernel(chips, block_ref, out_ref, send_sem, recv_sem, local_sem):
    me = lax.axis_index("dp")
    zz = lax.axis_index("zero")
    core = me % 2
    chip = me // 2
    sibling = me + 1 - 2 * core

    def peer(k):
        return ((chip + k) % chips) * 2 + core

    def source(k):
        return ((chip + chips - k) % chips) * 2 + core

    barrier = pltpu.get_barrier_semaphore()
    pl.semaphore_signal(barrier, inc=1, device_id=(sibling, zz), device_id_type=MESH)
    for k in range(1, chips):
        pl.semaphore_signal(barrier, inc=1, device_id=(peer(k), zz), device_id_type=MESH)
    pl.semaphore_wait(barrier, chips)

    local = pltpu.make_async_copy(block_ref, out_ref.at[me], local_sem)
    local.start()
    sends = []
    for k in range(1, chips):
        copy = pltpu.make_async_remote_copy(
            src_ref=block_ref,
            dst_ref=out_ref.at[me],
            send_sem=send_sem.at[k],
            recv_sem=recv_sem.at[me],
            device_id=(peer(k), zz),
            device_id_type=MESH,
        )
        copy.start()
        sends.append(copy)
    copy = pltpu.make_async_remote_copy(
        src_ref=block_ref,
        dst_ref=out_ref.at[me],
        send_sem=send_sem.at[0],
        recv_sem=recv_sem.at[me],
        device_id=(sibling, zz),
        device_id_type=MESH,
    )
    copy.start()
    sends.append(copy)
    for k in range(1, chips):
        s = source(k)
        arrived = pltpu.make_async_remote_copy(
            src_ref=out_ref.at[s],
            dst_ref=out_ref.at[s],
            send_sem=send_sem.at[chips + k],
            recv_sem=recv_sem.at[s],
            device_id=(sibling, zz),
            device_id_type=MESH,
        )
        arrived.wait_recv()
        arrived.start()
        sends.append(arrived)
    for k in range(chips):
        t = ((chip + k) % chips) * 2 + (1 - core)
        pltpu.make_async_remote_copy(
            src_ref=out_ref.at[t],
            dst_ref=out_ref.at[t],
            send_sem=send_sem.at[0],
            recv_sem=recv_sem.at[t],
            device_id=(sibling, zz),
            device_id_type=MESH,
        ).wait_recv()
    for copy in sends:
        copy.wait_send()
    local.wait()


def gather_dp(block):
    dp_size = lax.axis_size("dp")
    return pl.pallas_call(
        functools.partial(gather_kernel, dp_size // 2),
        out_shape=jax.ShapeDtypeStruct((dp_size,) + block.shape, block.dtype),
        in_specs=[pl.BlockSpec(memory_space=pl.ANY)],
        out_specs=pl.BlockSpec(memory_space=pl.ANY),
        scratch_shapes=[
            pltpu.SemaphoreType.DMA((dp_size,)),
            pltpu.SemaphoreType.DMA((dp_size,)),
            pltpu.SemaphoreType.DMA(()),
        ],
        compiler_params=pltpu.CompilerParams(collective_id=0, has_side_effects=True),
    )(block)


def tail_kernel(
    n, hidden_ref, sums_ref, hidden_out, slots_out,
    send_h, recv_h, send_d, recv_d, local_h, local_d,
):
    a = lax.axis_index("dp")
    b = lax.axis_index("zero")
    rows = hidden_ref.shape[0] // n
    cols = hidden_ref.shape[1]
    diagonal = a == b

    barrier = pltpu.get_barrier_semaphore()
    for j in range(1, n):
        pl.semaphore_signal(barrier, inc=1, device_id=((a + j) % n, b), device_id_type=MESH)
        pl.semaphore_signal(barrier, inc=1, device_id=((a + j) % n, a), device_id_type=MESH)
        pl.semaphore_signal(barrier, inc=1, device_id=(b, (b + j) % n), device_id_type=MESH)

    @pl.when(jnp.logical_not(diagonal))
    def _():
        pl.semaphore_signal(barrier, inc=1, device_id=(a, a), device_id_type=MESH)
        pl.semaphore_signal(barrier, inc=1, device_id=(b, b), device_id_type=MESH)

    pl.semaphore_wait(barrier, 3 * (n - 1) + 2 - 2 * diagonal.astype(jnp.int32))

    def hidden_copy(j):
        k = (a + j) % n
        return pltpu.make_async_remote_copy(
            src_ref=hidden_ref.at[pl.ds(pl.multiple_of(k * rows, rows), rows), :],
            dst_ref=hidden_out.at[:, pl.ds(pl.multiple_of(a * cols, cols), cols)],
            send_sem=send_h.at[j],
            recv_sem=recv_h.at[a],
            device_id=(k, b),
            device_id_type=MESH,
        )

    def sum_copy(j):
        k = (a + j) % n
        return pltpu.make_async_remote_copy(
            src_ref=sums_ref.at[k],
            dst_ref=slots_out.at[b],
            send_sem=send_d.at[j],
            recv_sem=recv_d.at[b],
            device_id=(k, a),
            device_id_type=MESH,
        )

    own_hidden = pltpu.make_async_copy(
        hidden_ref.at[pl.ds(pl.multiple_of(a * rows, rows), rows), :], hidden_out.at[:, pl.ds(pl.multiple_of(a * cols, cols), cols)], local_h
    )
    own_hidden.start()
    own_sum = pltpu.make_async_copy(sums_ref.at[a], slots_out.at[b], local_d)

    @pl.when(diagonal)
    def _():
        own_sum.start()

    @pl.when(jnp.logical_not(diagonal))
    def _():
        sum_copy(0).start()

    for j in range(1, n):
        hidden_copy(j).start()
        sum_copy(j).start()

    for j in range(1, n):
        k = (a + n - j) % n
        pltpu.make_async_remote_copy(
            src_ref=hidden_ref.at[pl.ds(0, rows), :],
            dst_ref=hidden_out.at[:, pl.ds(pl.multiple_of(k * cols, cols), cols)],
            send_sem=send_h.at[0],
            recv_sem=recv_h.at[k],
            device_id=(k, b),
            device_id_type=MESH,
        ).wait_recv()
        z = (b + j) % n
        pltpu.make_async_remote_copy(
            src_ref=sums_ref.at[0],
            dst_ref=slots_out.at[z],
            send_sem=send_d.at[0],
            recv_sem=recv_d.at[z],
            device_id=(b, z),
            device_id_type=MESH,
        ).wait_recv()

    @pl.when(diagonal)
    def _():
        own_sum.wait()

    @pl.when(jnp.logical_not(diagonal))
    def _():
        pltpu.make_async_remote_copy(
            src_ref=sums_ref.at[0],
            dst_ref=slots_out.at[b],
            send_sem=send_d.at[0],
            recv_sem=recv_d.at[b],
            device_id=(b, b),
            device_id_type=MESH,
        ).wait_recv()
        sum_copy(0).wait_send()

    for j in range(1, n):
        hidden_copy(j).wait_send()
        sum_copy(j).wait_send()
    own_hidden.wait()


def exchange_tail(hidden_part, group_sum):
    n = lax.axis_size("dp")
    rows = hidden_part.shape[0] // n
    return pl.pallas_call(
        functools.partial(tail_kernel, n),
        out_shape=(
            jax.ShapeDtypeStruct((rows, n * hidden_part.shape[1]), hidden_part.dtype),
            jax.ShapeDtypeStruct(group_sum.shape, group_sum.dtype),
        ),
        in_specs=[pl.BlockSpec(memory_space=pl.ANY)] * 2,
        out_specs=(pl.BlockSpec(memory_space=pl.ANY), pl.BlockSpec(memory_space=pl.ANY)),
        scratch_shapes=[pltpu.SemaphoreType.DMA((n,))] * 4 + [pltpu.SemaphoreType.DMA(())] * 2,
        compiler_params=pltpu.CompilerParams(collective_id=1, has_side_effects=True),
    )(hidden_part, group_sum)


def unit_rows(values):
    return values * lax.rsqrt(jnp.sum(values * values, axis=1, keepdims=True) + 1e-06)


def text_embed(features, closing_layernorm_multiplier):
    center = features - jnp.mean(features, axis=1, keepdims=True)
    spread = jnp.mean(center * center, axis=1, keepdims=True)
    return unit_rows(center * lax.rsqrt(spread + 1e-05) * closing_layernorm_multiplier)


def sigmoid_weights(scores, labels):
    return (-labels * jax.nn.sigmoid(-labels * scores)).astype(jnp.bfloat16)


def shards(
    picture_embeds,
    matched_slot,
    summary_token_states,
    feedforward_inner_activations,
    closing_layernorm_multiplier,
    contracting_matrix,
    sharpness_factor,
    additive_shift_learned,
):
    similarity_multiplier = sharpness_factor[0]
    shift_value = additive_shift_learned[0]
    local_rows, width = picture_embeds.shape

    dp_size = lax.axis_size("dp")
    zero_size = lax.axis_size("zero")
    dp_place = lax.axis_index("dp")
    own_start = dp_place * local_rows
    transpose_route = [
        (a * zero_size + b, b * zero_size + a) for a in range(dp_size) for b in range(zero_size)
    ]

    ffa_cols = lax.all_to_all(
        feedforward_inner_activations, "dp", split_axis=1, concat_axis=0, tiled=True
    )
    weight_block = lax.ppermute(contracting_matrix, ("dp", "zero"), transpose_route)

    digits = jnp.zeros((local_rows, 128), jnp.bfloat16)
    digits = digits.at[:, 0].set((matched_slot // 256).astype(jnp.bfloat16))
    digits = digits.at[:, 1].set((matched_slot % 256).astype(jnp.bfloat16))
    both = jnp.concatenate([picture_embeds, summary_token_states, digits], axis=1)
    both_g = gather_dp(both).reshape((-1, both.shape[1]))
    ffa_cols, weight_block, both_g = lax.optimization_barrier((ffa_cols, weight_block, both_g))
    digit_weights = jnp.zeros((128,), jnp.float32).at[0].set(256.0).at[1].set(1.0)
    slot_g = jnp.sum(
        both_g[:, 2 * width :].astype(jnp.float32) * digit_weights[None, :], axis=1
    ).astype(jnp.int32)
    image_b_g = unit_rows(both_g[:, :width].astype(jnp.float32)).astype(jnp.bfloat16)
    caption_g, caption_back = jax.vjp(
        lambda feats: text_embed(feats, closing_layernorm_multiplier),
        both_g[:, width : 2 * width].astype(jnp.float32),
    )
    caption_b_g = caption_g.astype(jnp.bfloat16)
    group_rows = caption_b_g.shape[0]

    unit_image, image_back = jax.vjp(unit_rows, picture_embeds.astype(jnp.float32))

    scores = (
        similarity_multiplier
        * lax.dot_general(
            image_b_g, caption_b_g, (((1,), (1,)), ((), ())), preferred_element_type=jnp.float32
        )
        + shift_value
    )
    places = jnp.arange(group_rows, dtype=jnp.int32)
    labels = jnp.where(slot_g[:, None] == places[None, :], 1.0, -1.0)
    weights = sigmoid_weights(scores, labels)
    own_weights = lax.dynamic_slice_in_dim(weights, own_start, local_rows, axis=0)
    image_term = similarity_multiplier * jnp.dot(
        own_weights, caption_b_g, preferred_element_type=jnp.float32
    )
    caption_term = similarity_multiplier * lax.dot_general(
        weights, image_b_g, (((0,), (0,)), ((), ())), preferred_element_type=jnp.float32
    )

    image_grad = image_back(image_term)[0]
    upstream_g = caption_back(caption_term)[0].astype(jnp.bfloat16)

    hidden_part = lax.dot_general(
        upstream_g,
        weight_block,
        (((1,), (1,)), ((), ())),
        preferred_element_type=jnp.float32,
    ).astype(jnp.bfloat16)
    group_sum = lax.dot_general(
        ffa_cols, upstream_g, (((0,), (0,)), ((), ())), preferred_element_type=jnp.float32
    )
    sum_slabs = group_sum.reshape((group_sum.shape[0], dp_size, -1)).transpose((1, 0, 2))
    hidden_grad, down_slots = exchange_tail(hidden_part, sum_slabs)
    down_grad = jnp.sum(down_slots, axis=0)
    return (image_grad, hidden_grad, down_grad)


def solution(mesh):
    placed = (
        P(("dp", "zero"), None),
        P(("dp", "zero")),
        P(("dp", "zero"), None),
        P(("dp", "zero"), None),
        P(),
        P("zero", None),
        P(),
        P(),
    )
    return jax.shard_map(
        shards,
        mesh=mesh,
        in_specs=placed,
        out_specs=(P(("dp", "zero"), None), P(("dp", "zero"), None), P("zero", "dp")),
        check_vma=False,
    )
```

```python
import functools

import jax
import jax.numpy as jnp
from jax import lax
from jax.experimental import pallas as pl
from jax.experimental.pallas import tpu as pltpu
from jax.sharding import PartitionSpec as P

MESH = pl.DeviceIdType.MESH


def gather_kernel(chips, block_ref, out_ref, send_sem, recv_sem, local_sem):
    me = lax.axis_index("dp")
    zz = lax.axis_index("zero")
    core = me % 2
    chip = me // 2
    sibling = me + 1 - 2 * core

    def peer(k):
        return ((chip + k) % chips) * 2 + core

    def source(k):
        return ((chip + chips - k) % chips) * 2 + core

    barrier = pltpu.get_barrier_semaphore()
    pl.semaphore_signal(barrier, inc=1, device_id=(sibling, zz), device_id_type=MESH)
    for k in range(1, chips):
        pl.semaphore_signal(barrier, inc=1, device_id=(peer(k), zz), device_id_type=MESH)
    pl.semaphore_wait(barrier, chips)

    local = pltpu.make_async_copy(block_ref, out_ref.at[me], local_sem)
    local.start()
    sends = []
    for k in range(1, chips):
        copy = pltpu.make_async_remote_copy(
            src_ref=block_ref,
            dst_ref=out_ref.at[me],
            send_sem=send_sem.at[k],
            recv_sem=recv_sem.at[me],
            device_id=(peer(k), zz),
            device_id_type=MESH,
        )
        copy.start()
        sends.append(copy)
    copy = pltpu.make_async_remote_copy(
        src_ref=block_ref,
        dst_ref=out_ref.at[me],
        send_sem=send_sem.at[0],
        recv_sem=recv_sem.at[me],
        device_id=(sibling, zz),
        device_id_type=MESH,
    )
    copy.start()
    sends.append(copy)
    for k in range(1, chips):
        s = source(k)
        arrived = pltpu.make_async_remote_copy(
            src_ref=out_ref.at[s],
            dst_ref=out_ref.at[s],
            send_sem=send_sem.at[chips + k],
            recv_sem=recv_sem.at[s],
            device_id=(sibling, zz),
            device_id_type=MESH,
        )
        arrived.wait_recv()
        arrived.start()
        sends.append(arrived)
    for k in range(chips):
        t = ((chip + k) % chips) * 2 + (1 - core)
        pltpu.make_async_remote_copy(
            src_ref=out_ref.at[t],
            dst_ref=out_ref.at[t],
            send_sem=send_sem.at[0],
            recv_sem=recv_sem.at[t],
            device_id=(sibling, zz),
            device_id_type=MESH,
        ).wait_recv()
    for copy in sends:
        copy.wait_send()
    local.wait()


def gather_dp(block):
    dp_size = lax.axis_size("dp")
    return pl.pallas_call(
        functools.partial(gather_kernel, dp_size // 2),
        out_shape=jax.ShapeDtypeStruct((dp_size,) + block.shape, block.dtype),
        in_specs=[pl.BlockSpec(memory_space=pl.ANY)],
        out_specs=pl.BlockSpec(memory_space=pl.ANY),
        scratch_shapes=[
            pltpu.SemaphoreType.DMA((dp_size,)),
            pltpu.SemaphoreType.DMA((dp_size,)),
            pltpu.SemaphoreType.DMA(()),
        ],
        compiler_params=pltpu.CompilerParams(collective_id=0, has_side_effects=True),
    )(block)


def tail_kernel(
    n, hidden_ref, sums_ref, hidden_out, slots_out,
    send_h, recv_h, send_d, recv_d, local_h, local_d,
):
    a = lax.axis_index("dp")
    b = lax.axis_index("zero")
    rows = hidden_out.shape[1]

    barrier = pltpu.get_barrier_semaphore()
    for j in range(1, n):
        pl.semaphore_signal(barrier, inc=1, device_id=((a + j) % n, b), device_id_type=MESH)
        pl.semaphore_signal(barrier, inc=1, device_id=(a, (b + j) % n), device_id_type=MESH)
    pl.semaphore_wait(barrier, 2 * (n - 1))

    def hidden_copy(j):
        k = (a + j) % n
        return pltpu.make_async_remote_copy(
            src_ref=hidden_ref.at[pl.ds(pl.multiple_of(k * rows, rows), rows), :],
            dst_ref=hidden_out.at[a],
            send_sem=send_h.at[j],
            recv_sem=recv_h.at[a],
            device_id=(k, b),
            device_id_type=MESH,
        )

    def sum_copy(j):
        k = (b + j) % n
        return pltpu.make_async_remote_copy(
            src_ref=sums_ref.at[k],
            dst_ref=slots_out.at[b],
            send_sem=send_d.at[j],
            recv_sem=recv_d.at[b],
            device_id=(a, k),
            device_id_type=MESH,
        )

    own_hidden = pltpu.make_async_copy(
        hidden_ref.at[pl.ds(pl.multiple_of(a * rows, rows), rows), :], hidden_out.at[a], local_h
    )
    own_sum = pltpu.make_async_copy(sums_ref.at[b], slots_out.at[b], local_d)
    own_hidden.start()
    own_sum.start()
    for j in range(1, n):
        sum_copy(j).start()
        hidden_copy(j).start()

    for j in range(1, n):
        k = (a + n - j) % n
        pltpu.make_async_remote_copy(
            src_ref=hidden_ref.at[pl.ds(0, rows), :],
            dst_ref=hidden_out.at[k],
            send_sem=send_h.at[0],
            recv_sem=recv_h.at[k],
            device_id=(k, b),
            device_id_type=MESH,
        ).wait_recv()
        z = (b + n - j) % n
        pltpu.make_async_remote_copy(
            src_ref=sums_ref.at[0],
            dst_ref=slots_out.at[z],
            send_sem=send_d.at[0],
            recv_sem=recv_d.at[z],
            device_id=(a, z),
            device_id_type=MESH,
        ).wait_recv()
    for j in range(1, n):
        hidden_copy(j).wait_send()
        sum_copy(j).wait_send()
    own_hidden.wait()
    own_sum.wait()


def exchange_tail(hidden_part, group_sum):
    n = lax.axis_size("dp")
    rows = hidden_part.shape[0] // n
    return pl.pallas_call(
        functools.partial(tail_kernel, n),
        out_shape=(
            jax.ShapeDtypeStruct((n, rows, hidden_part.shape[1]), hidden_part.dtype),
            jax.ShapeDtypeStruct(group_sum.shape, group_sum.dtype),
        ),
        in_specs=[pl.BlockSpec(memory_space=pl.ANY)] * 2,
        out_specs=(pl.BlockSpec(memory_space=pl.ANY), pl.BlockSpec(memory_space=pl.ANY)),
        scratch_shapes=[pltpu.SemaphoreType.DMA((n,))] * 4 + [pltpu.SemaphoreType.DMA(())] * 2,
        compiler_params=pltpu.CompilerParams(collective_id=1, has_side_effects=True),
    )(hidden_part, group_sum)


def unit_rows(values):
    return values * lax.rsqrt(jnp.sum(values * values, axis=1, keepdims=True) + 1e-06)


def text_embed(features, closing_layernorm_multiplier):
    center = features - jnp.mean(features, axis=1, keepdims=True)
    spread = jnp.mean(center * center, axis=1, keepdims=True)
    return unit_rows(center * lax.rsqrt(spread + 1e-05) * closing_layernorm_multiplier)


def sigmoid_weights(scores, labels):
    return (-labels * jax.nn.sigmoid(-labels * scores)).astype(jnp.bfloat16)


def shards(
    picture_embeds,
    matched_slot,
    summary_token_states,
    feedforward_inner_activations,
    closing_layernorm_multiplier,
    contracting_matrix,
    sharpness_factor,
    additive_shift_learned,
):
    similarity_multiplier = sharpness_factor[0]
    shift_value = additive_shift_learned[0]
    local_rows, width = picture_embeds.shape

    dp_size = lax.axis_size("dp")
    zero_size = lax.axis_size("zero")
    dp_place = lax.axis_index("dp")
    own_start = dp_place * local_rows
    transpose_route = [
        (a * zero_size + b, b * zero_size + a) for a in range(dp_size) for b in range(zero_size)
    ]

    ffa_cols = lax.all_to_all(
        feedforward_inner_activations, "dp", split_axis=1, concat_axis=0, tiled=True
    )
    weight_block = lax.ppermute(contracting_matrix, ("dp", "zero"), transpose_route)

    digits = jnp.zeros((local_rows, 128), jnp.bfloat16)
    digits = digits.at[:, 0].set((matched_slot // 256).astype(jnp.bfloat16))
    digits = digits.at[:, 1].set((matched_slot % 256).astype(jnp.bfloat16))
    both = jnp.concatenate([picture_embeds, summary_token_states, digits], axis=1)
    both_g = gather_dp(both).reshape((-1, both.shape[1]))
    ffa_cols, weight_block, both_g = lax.optimization_barrier((ffa_cols, weight_block, both_g))
    digit_weights = jnp.zeros((128,), jnp.float32).at[0].set(256.0).at[1].set(1.0)
    slot_g = jnp.sum(
        both_g[:, 2 * width :].astype(jnp.float32) * digit_weights[None, :], axis=1
    ).astype(jnp.int32)
    image_b_g = unit_rows(both_g[:, :width].astype(jnp.float32)).astype(jnp.bfloat16)
    caption_g, caption_back = jax.vjp(
        lambda feats: text_embed(feats, closing_layernorm_multiplier),
        both_g[:, width : 2 * width].astype(jnp.float32),
    )
    caption_b_g = caption_g.astype(jnp.bfloat16)
    group_rows = caption_b_g.shape[0]

    unit_image, image_back = jax.vjp(unit_rows, picture_embeds.astype(jnp.float32))

    scores = (
        similarity_multiplier
        * lax.dot_general(
            image_b_g, caption_b_g, (((1,), (1,)), ((), ())), preferred_element_type=jnp.float32
        )
        + shift_value
    )
    places = jnp.arange(group_rows, dtype=jnp.int32)
    labels = jnp.where(slot_g[:, None] == places[None, :], 1.0, -1.0)
    weights = sigmoid_weights(scores, labels)
    own_weights = lax.dynamic_slice_in_dim(weights, own_start, local_rows, axis=0)
    image_term = similarity_multiplier * jnp.dot(
        own_weights, caption_b_g, preferred_element_type=jnp.float32
    )
    caption_term = similarity_multiplier * lax.dot_general(
        weights, image_b_g, (((0,), (0,)), ((), ())), preferred_element_type=jnp.float32
    )

    image_grad = image_back(image_term)[0]
    upstream_g = caption_back(caption_term)[0].astype(jnp.bfloat16)

    hidden_part = lax.dot_general(
        upstream_g,
        weight_block,
        (((1,), (1,)), ((), ())),
        preferred_element_type=jnp.float32,
    ).astype(jnp.bfloat16)
    group_sum = lax.dot_general(
        ffa_cols, upstream_g, (((0,), (0,)), ((), ())), preferred_element_type=jnp.float32
    )
    sum_slabs = group_sum.reshape((group_sum.shape[0], zero_size, -1)).transpose((1, 0, 2))
    hidden_slots, down_slots = exchange_tail(hidden_part, sum_slabs)
    hidden_grad = hidden_slots.transpose((1, 0, 2)).reshape((local_rows, -1))
    down_grad = lax.ppermute(jnp.sum(down_slots, axis=0), ("dp", "zero"), transpose_route)
    return (image_grad, hidden_grad, down_grad)


def solution(mesh):
    placed = (
        P(("dp", "zero"), None),
        P(("dp", "zero")),
        P(("dp", "zero"), None),
        P(("dp", "zero"), None),
        P(),
        P("zero", None),
        P(),
        P(),
    )
    return jax.shard_map(
        shards,
        mesh=mesh,
        in_specs=placed,
        out_specs=(P(("dp", "zero"), None), P(("dp", "zero"), None), P("zero", "dp")),
        check_vma=False,
    )
```

```python
import functools

import jax
import jax.numpy as jnp
from jax import lax
from jax.experimental import pallas as pl
from jax.experimental.pallas import tpu as pltpu
from jax.sharding import PartitionSpec as P

MESH = pl.DeviceIdType.MESH


def gather_kernel(chips, block_ref, out_ref, send_sem, recv_sem, local_sem):
    me = lax.axis_index("dp")
    zz = lax.axis_index("zero")
    core = me % 2
    chip = me // 2
    sibling = me + 1 - 2 * core

    def peer(k):
        return ((chip + k) % chips) * 2 + core

    def source(k):
        return ((chip + chips - k) % chips) * 2 + core

    barrier = pltpu.get_barrier_semaphore()
    pl.semaphore_signal(barrier, inc=1, device_id=(sibling, zz), device_id_type=MESH)
    for k in range(1, chips):
        pl.semaphore_signal(barrier, inc=1, device_id=(peer(k), zz), device_id_type=MESH)
    pl.semaphore_wait(barrier, chips)

    local = pltpu.make_async_copy(block_ref, out_ref.at[me], local_sem)
    local.start()
    sends = []
    for k in range(1, chips):
        copy = pltpu.make_async_remote_copy(
            src_ref=block_ref,
            dst_ref=out_ref.at[me],
            send_sem=send_sem.at[k],
            recv_sem=recv_sem.at[me],
            device_id=(peer(k), zz),
            device_id_type=MESH,
        )
        copy.start()
        sends.append(copy)
    copy = pltpu.make_async_remote_copy(
        src_ref=block_ref,
        dst_ref=out_ref.at[me],
        send_sem=send_sem.at[0],
        recv_sem=recv_sem.at[me],
        device_id=(sibling, zz),
        device_id_type=MESH,
    )
    copy.start()
    sends.append(copy)
    for k in range(1, chips):
        s = source(k)
        arrived = pltpu.make_async_remote_copy(
            src_ref=out_ref.at[s],
            dst_ref=out_ref.at[s],
            send_sem=send_sem.at[chips + k],
            recv_sem=recv_sem.at[s],
            device_id=(sibling, zz),
            device_id_type=MESH,
        )
        arrived.wait_recv()
        arrived.start()
        sends.append(arrived)
    for k in range(chips):
        t = ((chip + k) % chips) * 2 + (1 - core)
        pltpu.make_async_remote_copy(
            src_ref=out_ref.at[t],
            dst_ref=out_ref.at[t],
            send_sem=send_sem.at[0],
            recv_sem=recv_sem.at[t],
            device_id=(sibling, zz),
            device_id_type=MESH,
        ).wait_recv()
    for copy in sends:
        copy.wait_send()
    local.wait()


def gather_dp(block):
    dp_size = lax.axis_size("dp")
    return pl.pallas_call(
        functools.partial(gather_kernel, dp_size // 2),
        out_shape=jax.ShapeDtypeStruct((dp_size,) + block.shape, block.dtype),
        in_specs=[pl.BlockSpec(memory_space=pl.ANY)],
        out_specs=pl.BlockSpec(memory_space=pl.ANY),
        scratch_shapes=[
            pltpu.SemaphoreType.DMA((dp_size,)),
            pltpu.SemaphoreType.DMA((dp_size,)),
            pltpu.SemaphoreType.DMA(()),
        ],
        compiler_params=pltpu.CompilerParams(collective_id=0, has_side_effects=True),
    )(block)


def contrast_kernel(
    scale_ref, shift_ref, own_slot_ref, slot_ref, images_ref, captions_ref,
    caption_out, image_out,
):
    jb = pl.program_id(0)
    tc = captions_ref.shape[0]
    rows = own_slot_ref.shape[0]
    chunk = 512
    scale = scale_ref[0]
    shift = shift_ref[0]
    captions = captions_ref[...]
    places = jb * tc + lax.broadcasted_iota(jnp.int32, (tc, 1), 0)

    def weights_of(scores, positive):
        labels = jnp.where(positive, 1.0, -1.0)
        return (-labels * jax.nn.sigmoid(-labels * scores)).astype(jnp.bfloat16)

    def body(ib, acc):
        start = pl.multiple_of(ib * chunk, chunk)
        images = images_ref[pl.ds(start, chunk), :]
        scores = scale * lax.dot_general(
            captions, images, (((1,), (1,)), ((), ())), preferred_element_type=jnp.float32
        ) + shift
        weights = weights_of(scores, slot_ref[:, pl.ds(start, chunk)] == places)
        return acc + jnp.dot(weights, images, preferred_element_type=jnp.float32)

    acc = lax.fori_loop(
        0, images_ref.shape[0] // chunk, body, jnp.zeros(caption_out.shape, jnp.float32)
    )
    caption_out[...] = scale * acc

    own_start = pl.multiple_of(lax.axis_index("dp") * rows, rows)
    own = images_ref[pl.ds(own_start, rows), :]
    own_scores = scale * lax.dot_general(
        own, captions, (((1,), (1,)), ((), ())), preferred_element_type=jnp.float32
    ) + shift
    columns = jb * tc + lax.broadcasted_iota(jnp.int32, (1, tc), 1)
    own_weights = weights_of(own_scores, own_slot_ref[...] == columns)

    @pl.when(jb == 0)
    def _():
        image_out[...] = jnp.zeros_like(image_out)

    image_out[...] += scale * jnp.dot(own_weights, captions, preferred_element_type=jnp.float32)


def contrast_group(scale, shift, own_slot, slot_g, image_b_g, caption_b_g):
    group_rows, width = caption_b_g.shape
    rows = own_slot.shape[0]
    tc = 256
    return pl.pallas_call(
        contrast_kernel,
        grid=(group_rows // tc,),
        out_shape=(
            jax.ShapeDtypeStruct((group_rows, width), jnp.float32),
            jax.ShapeDtypeStruct((rows, width), jnp.float32),
        ),
        in_specs=[
            pl.BlockSpec(memory_space=pltpu.SMEM),
            pl.BlockSpec(memory_space=pltpu.SMEM),
            pl.BlockSpec((rows, 1), lambda j: (0, 0)),
            pl.BlockSpec((1, group_rows), lambda j: (0, 0)),
            pl.BlockSpec((group_rows, width), lambda j: (0, 0)),
            pl.BlockSpec((tc, width), lambda j: (j, 0)),
        ],
        out_specs=(
            pl.BlockSpec((tc, width), lambda j: (j, 0)),
            pl.BlockSpec((rows, width), lambda j: (0, 0)),
        ),
        compiler_params=pltpu.CompilerParams(dimension_semantics=("arbitrary",)),
        cost_estimate=pl.CostEstimate(
            flops=4 * group_rows * (group_rows + rows) * width,
            bytes_accessed=2 * group_rows * width * 2 + (group_rows + rows) * width * 4,
            transcendentals=group_rows * (group_rows + rows),
        ),
    )(scale, shift, own_slot.reshape((rows, 1)), slot_g.reshape((1, group_rows)), image_b_g, caption_b_g)


def unit_rows(values):
    return values * lax.rsqrt(jnp.sum(values * values, axis=1, keepdims=True) + 1e-06)


def text_embed(features, closing_layernorm_multiplier):
    center = features - jnp.mean(features, axis=1, keepdims=True)
    spread = jnp.mean(center * center, axis=1, keepdims=True)
    return unit_rows(center * lax.rsqrt(spread + 1e-05) * closing_layernorm_multiplier)


def sigmoid_weights(scores, labels):
    return (-labels * jax.nn.sigmoid(-labels * scores)).astype(jnp.bfloat16)


def shards(
    picture_embeds,
    matched_slot,
    summary_token_states,
    feedforward_inner_activations,
    closing_layernorm_multiplier,
    contracting_matrix,
    sharpness_factor,
    additive_shift_learned,
):
    similarity_multiplier = sharpness_factor[0]
    shift_value = additive_shift_learned[0]
    local_rows, width = picture_embeds.shape

    dp_size = lax.axis_size("dp")
    zero_size = lax.axis_size("zero")
    dp_place = lax.axis_index("dp")
    own_start = dp_place * local_rows
    transpose_route = [
        (a * zero_size + b, b * zero_size + a) for a in range(dp_size) for b in range(zero_size)
    ]

    ffa_cols = lax.all_to_all(
        feedforward_inner_activations, "dp", split_axis=1, concat_axis=0, tiled=True
    )
    weight_block = lax.ppermute(contracting_matrix, ("dp", "zero"), transpose_route)

    digits = jnp.zeros((local_rows, 128), jnp.bfloat16)
    digits = digits.at[:, 0].set((matched_slot // 256).astype(jnp.bfloat16))
    digits = digits.at[:, 1].set((matched_slot % 256).astype(jnp.bfloat16))
    both = jnp.concatenate([picture_embeds, summary_token_states, digits], axis=1)
    both_g = gather_dp(both).reshape((-1, both.shape[1]))
    ffa_cols, weight_block, both_g = lax.optimization_barrier((ffa_cols, weight_block, both_g))
    slot_g = both_g[:, 2 * width].astype(jnp.int32) * 256 + both_g[:, 2 * width + 1].astype(
        jnp.int32
    )
    image_b_g = unit_rows(both_g[:, :width].astype(jnp.float32)).astype(jnp.bfloat16)
    caption_g, caption_back = jax.vjp(
        lambda feats: text_embed(feats, closing_layernorm_multiplier),
        both_g[:, width : 2 * width].astype(jnp.float32),
    )
    caption_b_g = caption_g.astype(jnp.bfloat16)
    group_rows = caption_b_g.shape[0]

    unit_image, image_back = jax.vjp(unit_rows, picture_embeds.astype(jnp.float32))

    caption_term, image_term = contrast_group(
        sharpness_factor, additive_shift_learned, matched_slot, slot_g, image_b_g, caption_b_g
    )

    image_grad = image_back(image_term)[0]
    upstream_g = caption_back(caption_term)[0].astype(jnp.bfloat16)

    hidden_part = lax.dot_general(
        upstream_g,
        weight_block,
        (((1,), (1,)), ((), ())),
        preferred_element_type=jnp.float32,
    ).astype(jnp.bfloat16)
    hidden_grad = lax.all_to_all(hidden_part, "dp", split_axis=0, concat_axis=1, tiled=True)
    group_sum = lax.dot_general(
        ffa_cols, upstream_g, (((0,), (0,)), ((), ())), preferred_element_type=jnp.float32
    )
    down_parts = lax.all_to_all(group_sum, "zero", split_axis=1, concat_axis=0, tiled=True)
    down_block = jnp.sum(down_parts.reshape((zero_size,) + (group_sum.shape[0], -1)), axis=0)
    down_grad = lax.ppermute(down_block, ("dp", "zero"), transpose_route)
    return (image_grad, hidden_grad, down_grad)


def solution(mesh):
    placed = (
        P(("dp", "zero"), None),
        P(("dp", "zero")),
        P(("dp", "zero"), None),
        P(("dp", "zero"), None),
        P(),
        P("zero", None),
        P(),
        P(),
    )
    return jax.shard_map(
        shards,
        mesh=mesh,
        in_specs=placed,
        out_specs=(P(("dp", "zero"), None), P(("dp", "zero"), None), P("zero", "dp")),
        check_vma=False,
    )
```

```python
import functools

import jax
import jax.numpy as jnp
from jax import lax
from jax.experimental import pallas as pl
from jax.experimental.pallas import tpu as pltpu
from jax.sharding import PartitionSpec as P

MESH = pl.DeviceIdType.MESH


def gather_kernel(chips, block_ref, out_ref, send_sem, recv_sem, local_sem):
    me = lax.axis_index("dp")
    zz = lax.axis_index("zero")
    core = me % 2
    chip = me // 2
    sibling = me + 1 - 2 * core

    def peer(k):
        return ((chip + k) % chips) * 2 + core

    def source(k):
        return ((chip + chips - k) % chips) * 2 + core

    barrier = pltpu.get_barrier_semaphore()
    pl.semaphore_signal(barrier, inc=1, device_id=(sibling, zz), device_id_type=MESH)
    for k in range(1, chips):
        pl.semaphore_signal(barrier, inc=1, device_id=(peer(k), zz), device_id_type=MESH)
    pl.semaphore_wait(barrier, chips)

    local = pltpu.make_async_copy(block_ref, out_ref.at[me], local_sem)
    local.start()
    sends = []
    for k in range(1, chips):
        copy = pltpu.make_async_remote_copy(
            src_ref=block_ref,
            dst_ref=out_ref.at[me],
            send_sem=send_sem.at[k],
            recv_sem=recv_sem.at[me],
            device_id=(peer(k), zz),
            device_id_type=MESH,
        )
        copy.start()
        sends.append(copy)
    copy = pltpu.make_async_remote_copy(
        src_ref=block_ref,
        dst_ref=out_ref.at[me],
        send_sem=send_sem.at[0],
        recv_sem=recv_sem.at[me],
        device_id=(sibling, zz),
        device_id_type=MESH,
    )
    copy.start()
    sends.append(copy)
    for k in range(1, chips):
        s = source(k)
        arrived = pltpu.make_async_remote_copy(
            src_ref=out_ref.at[s],
            dst_ref=out_ref.at[s],
            send_sem=send_sem.at[chips + k],
            recv_sem=recv_sem.at[s],
            device_id=(sibling, zz),
            device_id_type=MESH,
        )
        arrived.wait_recv()
        arrived.start()
        sends.append(arrived)
    for k in range(chips):
        t = ((chip + k) % chips) * 2 + (1 - core)
        pltpu.make_async_remote_copy(
            src_ref=out_ref.at[t],
            dst_ref=out_ref.at[t],
            send_sem=send_sem.at[0],
            recv_sem=recv_sem.at[t],
            device_id=(sibling, zz),
            device_id_type=MESH,
        ).wait_recv()
    for copy in sends:
        copy.wait_send()
    local.wait()


def gather_dp(block):
    dp_size = lax.axis_size("dp")
    return pl.pallas_call(
        functools.partial(gather_kernel, dp_size // 2),
        out_shape=jax.ShapeDtypeStruct((dp_size,) + block.shape, block.dtype),
        in_specs=[pl.BlockSpec(memory_space=pl.ANY)],
        out_specs=pl.BlockSpec(memory_space=pl.ANY),
        scratch_shapes=[
            pltpu.SemaphoreType.DMA((dp_size,)),
            pltpu.SemaphoreType.DMA((dp_size,)),
            pltpu.SemaphoreType.DMA(()),
        ],
        compiler_params=pltpu.CompilerParams(collective_id=0, has_side_effects=True),
    )(block)


def contrast_kernel(
    scale_ref, shift_ref, own_slot_ref, slot_ref, images_ref, images_t_ref, captions_ref,
    caption_out, image_out,
):
    jb = pl.program_id(0)
    tc = captions_ref.shape[0]
    rows = own_slot_ref.shape[1]
    chunk = 512
    scale = scale_ref[0]
    shift = shift_ref[0]
    captions = captions_ref[...]
    places = jb * tc + lax.broadcasted_iota(jnp.int32, (tc, 1), 0)

    def weights_of(scores, positive):
        labels = jnp.where(positive, 1.0, -1.0)
        return (-labels * jax.nn.sigmoid(-labels * scores)).astype(jnp.bfloat16)

    def body(ib, acc):
        start = pl.multiple_of(ib * chunk, chunk)
        images = images_ref[pl.ds(start, chunk), :]
        scores = scale * jnp.dot(
            captions, images_t_ref[:, pl.ds(start, chunk)], preferred_element_type=jnp.float32
        ) + shift
        weights = weights_of(scores, slot_ref[:, pl.ds(start, chunk)] == places)
        return acc + jnp.dot(weights, images, preferred_element_type=jnp.float32)

    acc = lax.fori_loop(
        0, images_ref.shape[0] // chunk, body, jnp.zeros(caption_out.shape, jnp.float32)
    )
    caption_out[...] = scale * acc

    own_start = pl.multiple_of(lax.axis_index("dp") * rows, rows)
    own_scores = scale * jnp.dot(
        captions, images_t_ref[:, pl.ds(own_start, rows)], preferred_element_type=jnp.float32
    ) + shift
    own_weights = weights_of(own_scores, own_slot_ref[...] == places)

    @pl.when(jb == 0)
    def _():
        image_out[...] = jnp.zeros_like(image_out)

    image_out[...] += scale * jnp.dot(
        own_weights.T, captions, preferred_element_type=jnp.float32
    )


def contrast_group(scale, shift, own_slot, slot_g, image_b_g, caption_b_g):
    group_rows, width = caption_b_g.shape
    rows = own_slot.shape[0]
    tc = 256
    return pl.pallas_call(
        contrast_kernel,
        grid=(group_rows // tc,),
        out_shape=(
            jax.ShapeDtypeStruct((group_rows, width), jnp.float32),
            jax.ShapeDtypeStruct((rows, width), jnp.float32),
        ),
        in_specs=[
            pl.BlockSpec(memory_space=pltpu.SMEM),
            pl.BlockSpec(memory_space=pltpu.SMEM),
            pl.BlockSpec((1, rows), lambda j: (0, 0)),
            pl.BlockSpec((1, group_rows), lambda j: (0, 0)),
            pl.BlockSpec((group_rows, width), lambda j: (0, 0)),
            pl.BlockSpec((width, group_rows), lambda j: (0, 0)),
            pl.BlockSpec((tc, width), lambda j: (j, 0)),
        ],
        out_specs=(
            pl.BlockSpec((tc, width), lambda j: (j, 0)),
            pl.BlockSpec((rows, width), lambda j: (0, 0)),
        ),
        compiler_params=pltpu.CompilerParams(dimension_semantics=("arbitrary",)),
        cost_estimate=pl.CostEstimate(
            flops=4 * group_rows * (group_rows + rows) * width,
            bytes_accessed=2 * group_rows * width * 2 + (group_rows + rows) * width * 4,
            transcendentals=group_rows * (group_rows + rows),
        ),
    )(
        scale,
        shift,
        own_slot.reshape((1, rows)),
        slot_g.reshape((1, group_rows)),
        image_b_g,
        image_b_g.T,
        caption_b_g,
    )


def unit_rows(values):
    return values * lax.rsqrt(jnp.sum(values * values, axis=1, keepdims=True) + 1e-06)


def text_embed(features, closing_layernorm_multiplier):
    center = features - jnp.mean(features, axis=1, keepdims=True)
    spread = jnp.mean(center * center, axis=1, keepdims=True)
    return unit_rows(center * lax.rsqrt(spread + 1e-05) * closing_layernorm_multiplier)


def sigmoid_weights(scores, labels):
    return (-labels * jax.nn.sigmoid(-labels * scores)).astype(jnp.bfloat16)


def shards(
    picture_embeds,
    matched_slot,
    summary_token_states,
    feedforward_inner_activations,
    closing_layernorm_multiplier,
    contracting_matrix,
    sharpness_factor,
    additive_shift_learned,
):
    similarity_multiplier = sharpness_factor[0]
    shift_value = additive_shift_learned[0]
    local_rows, width = picture_embeds.shape

    dp_size = lax.axis_size("dp")
    zero_size = lax.axis_size("zero")
    dp_place = lax.axis_index("dp")
    own_start = dp_place * local_rows
    transpose_route = [
        (a * zero_size + b, b * zero_size + a) for a in range(dp_size) for b in range(zero_size)
    ]

    ffa_cols = lax.all_to_all(
        feedforward_inner_activations, "dp", split_axis=1, concat_axis=0, tiled=True
    )
    weight_block = lax.ppermute(contracting_matrix, ("dp", "zero"), transpose_route)

    digits = jnp.zeros((local_rows, 128), jnp.bfloat16)
    digits = digits.at[:, 0].set((matched_slot // 256).astype(jnp.bfloat16))
    digits = digits.at[:, 1].set((matched_slot % 256).astype(jnp.bfloat16))
    both = jnp.concatenate([picture_embeds, summary_token_states, digits], axis=1)
    both_g = gather_dp(both).reshape((-1, both.shape[1]))
    ffa_cols, weight_block, both_g = lax.optimization_barrier((ffa_cols, weight_block, both_g))
    slot_g = both_g[:, 2 * width].astype(jnp.int32) * 256 + both_g[:, 2 * width + 1].astype(
        jnp.int32
    )
    image_b_g = unit_rows(both_g[:, :width].astype(jnp.float32)).astype(jnp.bfloat16)
    caption_g, caption_back = jax.vjp(
        lambda feats: text_embed(feats, closing_layernorm_multiplier),
        both_g[:, width : 2 * width].astype(jnp.float32),
    )
    caption_b_g = caption_g.astype(jnp.bfloat16)
    group_rows = caption_b_g.shape[0]

    unit_image, image_back = jax.vjp(unit_rows, picture_embeds.astype(jnp.float32))

    caption_term, image_term = contrast_group(
        sharpness_factor, additive_shift_learned, matched_slot, slot_g, image_b_g, caption_b_g
    )

    image_grad = image_back(image_term)[0]
    upstream_g = caption_back(caption_term)[0].astype(jnp.bfloat16)

    hidden_part = lax.dot_general(
        upstream_g,
        weight_block,
        (((1,), (1,)), ((), ())),
        preferred_element_type=jnp.float32,
    ).astype(jnp.bfloat16)
    hidden_grad = lax.all_to_all(hidden_part, "dp", split_axis=0, concat_axis=1, tiled=True)
    group_sum = lax.dot_general(
        ffa_cols, upstream_g, (((0,), (0,)), ((), ())), preferred_element_type=jnp.float32
    )
    down_parts = lax.all_to_all(group_sum, "zero", split_axis=1, concat_axis=0, tiled=True)
    down_block = jnp.sum(down_parts.reshape((zero_size,) + (group_sum.shape[0], -1)), axis=0)
    down_grad = lax.ppermute(down_block, ("dp", "zero"), transpose_route)
    return (image_grad, hidden_grad, down_grad)


def solution(mesh):
    placed = (
        P(("dp", "zero"), None),
        P(("dp", "zero")),
        P(("dp", "zero"), None),
        P(("dp", "zero"), None),
        P(),
        P("zero", None),
        P(),
        P(),
    )
    return jax.shard_map(
        shards,
        mesh=mesh,
        in_specs=placed,
        out_specs=(P(("dp", "zero"), None), P(("dp", "zero"), None), P("zero", "dp")),
        check_vma=False,
    )
```

```python
import functools

import jax
import jax.numpy as jnp
from jax import lax
from jax.experimental import pallas as pl
from jax.experimental.pallas import tpu as pltpu
from jax.sharding import PartitionSpec as P

MESH = pl.DeviceIdType.MESH


def gather_kernel(chips, block_ref, out_ref, send_sem, recv_sem, local_sem):
    me = lax.axis_index("dp")
    zz = lax.axis_index("zero")
    core = me % 2
    chip = me // 2
    sibling = me + 1 - 2 * core

    def peer(k):
        return ((chip + k) % chips) * 2 + core

    def source(k):
        return ((chip + chips - k) % chips) * 2 + core

    barrier = pltpu.get_barrier_semaphore()
    pl.semaphore_signal(barrier, inc=1, device_id=(sibling, zz), device_id_type=MESH)
    for k in range(1, chips):
        pl.semaphore_signal(barrier, inc=1, device_id=(peer(k), zz), device_id_type=MESH)
    pl.semaphore_wait(barrier, chips)

    local = pltpu.make_async_copy(block_ref, out_ref.at[me], local_sem)
    local.start()
    sends = []
    for k in range(1, chips):
        copy = pltpu.make_async_remote_copy(
            src_ref=block_ref,
            dst_ref=out_ref.at[me],
            send_sem=send_sem.at[k],
            recv_sem=recv_sem.at[me],
            device_id=(peer(k), zz),
            device_id_type=MESH,
        )
        copy.start()
        sends.append(copy)
    copy = pltpu.make_async_remote_copy(
        src_ref=block_ref,
        dst_ref=out_ref.at[me],
        send_sem=send_sem.at[0],
        recv_sem=recv_sem.at[me],
        device_id=(sibling, zz),
        device_id_type=MESH,
    )
    copy.start()
    sends.append(copy)
    for k in range(1, chips):
        s = source(k)
        arrived = pltpu.make_async_remote_copy(
            src_ref=out_ref.at[s],
            dst_ref=out_ref.at[s],
            send_sem=send_sem.at[chips + k],
            recv_sem=recv_sem.at[s],
            device_id=(sibling, zz),
            device_id_type=MESH,
        )
        arrived.wait_recv()
        arrived.start()
        sends.append(arrived)
    for k in range(chips):
        t = ((chip + k) % chips) * 2 + (1 - core)
        pltpu.make_async_remote_copy(
            src_ref=out_ref.at[t],
            dst_ref=out_ref.at[t],
            send_sem=send_sem.at[0],
            recv_sem=recv_sem.at[t],
            device_id=(sibling, zz),
            device_id_type=MESH,
        ).wait_recv()
    for copy in sends:
        copy.wait_send()
    local.wait()


def gather_dp(block):
    dp_size = lax.axis_size("dp")
    return pl.pallas_call(
        functools.partial(gather_kernel, dp_size // 2),
        out_shape=jax.ShapeDtypeStruct((dp_size,) + block.shape, block.dtype),
        in_specs=[pl.BlockSpec(memory_space=pl.ANY)],
        out_specs=pl.BlockSpec(memory_space=pl.ANY),
        scratch_shapes=[
            pltpu.SemaphoreType.DMA((dp_size,)),
            pltpu.SemaphoreType.DMA((dp_size,)),
            pltpu.SemaphoreType.DMA(()),
        ],
        compiler_params=pltpu.CompilerParams(collective_id=0, has_side_effects=True),
    )(block)


def contrast_kernel(
    scale_ref, shift_ref, own_slot_ref, slot_ref, images_ref, captions_ref,
    caption_out, image_out,
):
    jb = pl.program_id(0)
    tc = captions_ref.shape[0]
    rows = own_slot_ref.shape[0]
    chunk = 512
    scale = scale_ref[0]
    half_scale = 0.5 * scale
    half_shift = 0.5 * shift_ref[0]
    captions = captions_ref[...]
    places = jb * tc + lax.broadcasted_iota(jnp.int32, (tc, 1), 0)

    def weights_of(products, positive):
        half = 0.5 * jnp.tanh(half_scale * products + half_shift)
        return jnp.where(positive, half - 0.5, half + 0.5).astype(jnp.bfloat16)

    def body(ib, acc):
        start = pl.multiple_of(ib * chunk, chunk)
        images = images_ref[pl.ds(start, chunk), :]
        products = lax.dot_general(
            captions, images, (((1,), (1,)), ((), ())), preferred_element_type=jnp.float32
        )
        weights = weights_of(products, slot_ref[:, pl.ds(start, chunk)] == places)
        return acc + jnp.dot(weights, images, preferred_element_type=jnp.float32)

    acc = lax.fori_loop(
        0, images_ref.shape[0] // chunk, body, jnp.zeros(caption_out.shape, jnp.float32)
    )
    caption_out[...] = scale * acc

    own_start = pl.multiple_of(lax.axis_index("dp") * rows, rows)
    own = images_ref[pl.ds(own_start, rows), :]
    own_scores = lax.dot_general(
        own, captions, (((1,), (1,)), ((), ())), preferred_element_type=jnp.float32
    )
    columns = jb * tc + lax.broadcasted_iota(jnp.int32, (1, tc), 1)
    own_weights = weights_of(own_scores, own_slot_ref[...] == columns)

    @pl.when(jb == 0)
    def _():
        image_out[...] = jnp.zeros_like(image_out)

    image_out[...] += scale * jnp.dot(own_weights, captions, preferred_element_type=jnp.float32)


def contrast_group(scale, shift, own_slot, slot_g, image_b_g, caption_b_g):
    group_rows, width = caption_b_g.shape
    rows = own_slot.shape[0]
    tc = 256
    return pl.pallas_call(
        contrast_kernel,
        grid=(group_rows // tc,),
        out_shape=(
            jax.ShapeDtypeStruct((group_rows, width), jnp.float32),
            jax.ShapeDtypeStruct((rows, width), jnp.float32),
        ),
        in_specs=[
            pl.BlockSpec(memory_space=pltpu.SMEM),
            pl.BlockSpec(memory_space=pltpu.SMEM),
            pl.BlockSpec((rows, 1), lambda j: (0, 0)),
            pl.BlockSpec((1, group_rows), lambda j: (0, 0)),
            pl.BlockSpec((group_rows, width), lambda j: (0, 0)),
            pl.BlockSpec((tc, width), lambda j: (j, 0)),
        ],
        out_specs=(
            pl.BlockSpec((tc, width), lambda j: (j, 0)),
            pl.BlockSpec((rows, width), lambda j: (0, 0)),
        ),
        compiler_params=pltpu.CompilerParams(dimension_semantics=("arbitrary",)),
        cost_estimate=pl.CostEstimate(
            flops=4 * group_rows * (group_rows + rows) * width,
            bytes_accessed=2 * group_rows * width * 2 + (group_rows + rows) * width * 4,
            transcendentals=group_rows * (group_rows + rows),
        ),
    )(scale, shift, own_slot.reshape((rows, 1)), slot_g.reshape((1, group_rows)), image_b_g, caption_b_g)


def unit_rows(values):
    return values * lax.rsqrt(jnp.sum(values * values, axis=1, keepdims=True) + 1e-06)


def text_embed(features, closing_layernorm_multiplier):
    center = features - jnp.mean(features, axis=1, keepdims=True)
    spread = jnp.mean(center * center, axis=1, keepdims=True)
    return unit_rows(center * lax.rsqrt(spread + 1e-05) * closing_layernorm_multiplier)


def sigmoid_weights(scores, labels):
    return (-labels * jax.nn.sigmoid(-labels * scores)).astype(jnp.bfloat16)


def shards(
    picture_embeds,
    matched_slot,
    summary_token_states,
    feedforward_inner_activations,
    closing_layernorm_multiplier,
    contracting_matrix,
    sharpness_factor,
    additive_shift_learned,
):
    similarity_multiplier = sharpness_factor[0]
    shift_value = additive_shift_learned[0]
    local_rows, width = picture_embeds.shape

    dp_size = lax.axis_size("dp")
    zero_size = lax.axis_size("zero")
    dp_place = lax.axis_index("dp")
    own_start = dp_place * local_rows
    transpose_route = [
        (a * zero_size + b, b * zero_size + a) for a in range(dp_size) for b in range(zero_size)
    ]

    ffa_cols = lax.all_to_all(
        feedforward_inner_activations, "dp", split_axis=1, concat_axis=0, tiled=True
    )
    weight_block = lax.ppermute(contracting_matrix, ("dp", "zero"), transpose_route)

    digits = jnp.zeros((local_rows, 128), jnp.bfloat16)
    digits = digits.at[:, 0].set((matched_slot // 256).astype(jnp.bfloat16))
    digits = digits.at[:, 1].set((matched_slot % 256).astype(jnp.bfloat16))
    both = jnp.concatenate([picture_embeds, summary_token_states, digits], axis=1)
    both_g = gather_dp(both).reshape((-1, both.shape[1]))
    ffa_cols, weight_block, both_g = lax.optimization_barrier((ffa_cols, weight_block, both_g))
    slot_g = both_g[:, 2 * width].astype(jnp.int32) * 256 + both_g[:, 2 * width + 1].astype(
        jnp.int32
    )
    image_b_g = unit_rows(both_g[:, :width].astype(jnp.float32)).astype(jnp.bfloat16)
    caption_g, caption_back = jax.vjp(
        lambda feats: text_embed(feats, closing_layernorm_multiplier),
        both_g[:, width : 2 * width].astype(jnp.float32),
    )
    caption_b_g = caption_g.astype(jnp.bfloat16)
    group_rows = caption_b_g.shape[0]

    unit_image, image_back = jax.vjp(unit_rows, picture_embeds.astype(jnp.float32))

    caption_term, image_term = contrast_group(
        sharpness_factor, additive_shift_learned, matched_slot, slot_g, image_b_g, caption_b_g
    )

    image_grad = image_back(image_term)[0]
    upstream_g = caption_back(caption_term)[0].astype(jnp.bfloat16)

    hidden_part = lax.dot_general(
        upstream_g,
        weight_block,
        (((1,), (1,)), ((), ())),
        preferred_element_type=jnp.float32,
    ).astype(jnp.bfloat16)
    hidden_grad = lax.all_to_all(hidden_part, "dp", split_axis=0, concat_axis=1, tiled=True)
    group_sum = lax.dot_general(
        ffa_cols, upstream_g, (((0,), (0,)), ((), ())), preferred_element_type=jnp.float32
    )
    down_parts = lax.all_to_all(group_sum, "zero", split_axis=1, concat_axis=0, tiled=True)
    down_block = jnp.sum(down_parts.reshape((zero_size,) + (group_sum.shape[0], -1)), axis=0)
    down_grad = lax.ppermute(down_block, ("dp", "zero"), transpose_route)
    return (image_grad, hidden_grad, down_grad)


def solution(mesh):
    placed = (
        P(("dp", "zero"), None),
        P(("dp", "zero")),
        P(("dp", "zero"), None),
        P(("dp", "zero"), None),
        P(),
        P("zero", None),
        P(),
        P(),
    )
    return jax.shard_map(
        shards,
        mesh=mesh,
        in_specs=placed,
        out_specs=(P(("dp", "zero"), None), P(("dp", "zero"), None), P("zero", "dp")),
        check_vma=False,
    )
```

```python
import functools

import jax
import jax.numpy as jnp
from jax import lax
from jax.experimental import pallas as pl
from jax.experimental.pallas import tpu as pltpu
from jax.sharding import PartitionSpec as P

MESH = pl.DeviceIdType.MESH


def gather_kernel(chips, block_ref, out_ref, send_sem, recv_sem, local_sem):
    me = lax.axis_index("dp")
    zz = lax.axis_index("zero")
    core = me % 2
    chip = me // 2
    sibling = me + 1 - 2 * core

    def peer(k):
        return ((chip + k) % chips) * 2 + core

    def source(k):
        return ((chip + chips - k) % chips) * 2 + core

    barrier = pltpu.get_barrier_semaphore()
    pl.semaphore_signal(barrier, inc=1, device_id=(sibling, zz), device_id_type=MESH)
    for k in range(1, chips):
        pl.semaphore_signal(barrier, inc=1, device_id=(peer(k), zz), device_id_type=MESH)
    pl.semaphore_wait(barrier, chips)

    local = pltpu.make_async_copy(block_ref, out_ref.at[me], local_sem)
    local.start()
    sends = []
    for k in range(1, chips):
        copy = pltpu.make_async_remote_copy(
            src_ref=block_ref,
            dst_ref=out_ref.at[me],
            send_sem=send_sem.at[k],
            recv_sem=recv_sem.at[me],
            device_id=(peer(k), zz),
            device_id_type=MESH,
        )
        copy.start()
        sends.append(copy)
    copy = pltpu.make_async_remote_copy(
        src_ref=block_ref,
        dst_ref=out_ref.at[me],
        send_sem=send_sem.at[0],
        recv_sem=recv_sem.at[me],
        device_id=(sibling, zz),
        device_id_type=MESH,
    )
    copy.start()
    sends.append(copy)
    for k in range(1, chips):
        s = source(k)
        arrived = pltpu.make_async_remote_copy(
            src_ref=out_ref.at[s],
            dst_ref=out_ref.at[s],
            send_sem=send_sem.at[chips + k],
            recv_sem=recv_sem.at[s],
            device_id=(sibling, zz),
            device_id_type=MESH,
        )
        arrived.wait_recv()
        arrived.start()
        sends.append(arrived)
    for k in range(chips):
        t = ((chip + k) % chips) * 2 + (1 - core)
        pltpu.make_async_remote_copy(
            src_ref=out_ref.at[t],
            dst_ref=out_ref.at[t],
            send_sem=send_sem.at[0],
            recv_sem=recv_sem.at[t],
            device_id=(sibling, zz),
            device_id_type=MESH,
        ).wait_recv()
    for copy in sends:
        copy.wait_send()
    local.wait()


def gather_dp(block):
    dp_size = lax.axis_size("dp")
    return pl.pallas_call(
        functools.partial(gather_kernel, dp_size // 2),
        out_shape=jax.ShapeDtypeStruct((dp_size,) + block.shape, block.dtype),
        in_specs=[pl.BlockSpec(memory_space=pl.ANY)],
        out_specs=pl.BlockSpec(memory_space=pl.ANY),
        scratch_shapes=[
            pltpu.SemaphoreType.DMA((dp_size,)),
            pltpu.SemaphoreType.DMA((dp_size,)),
            pltpu.SemaphoreType.DMA(()),
        ],
        compiler_params=pltpu.CompilerParams(collective_id=0, has_side_effects=True),
    )(block)


def contrast_kernel(
    scale_ref, shift_ref, own_slot_ref, slot_ref, images_ref, captions_ref,
    caption_out, image_out,
):
    jb = pl.program_id(0)
    tc = captions_ref.shape[0]
    rows = own_slot_ref.shape[0]
    scale = scale_ref[0]
    half_scale = 0.5 * scale
    half_shift = 0.5 * shift_ref[0]
    captions = captions_ref[...]
    places = jb * tc + lax.broadcasted_iota(jnp.int32, (tc, 1), 0)

    def weights_of(products, positive):
        half = 0.5 * jnp.tanh(half_scale * products + half_shift)
        return jnp.where(positive, half - 0.5, half + 0.5).astype(jnp.bfloat16)

    images = images_ref[...]
    products = lax.dot_general(
        captions, images, (((1,), (1,)), ((), ())), preferred_element_type=jnp.float32
    )
    weights = weights_of(products, slot_ref[...] == places)
    acc = jnp.dot(weights, images, preferred_element_type=jnp.float32)
    caption_out[...] = scale * acc

    own_start = pl.multiple_of(lax.axis_index("dp") * rows, rows)
    own = images_ref[pl.ds(own_start, rows), :]
    own_scores = lax.dot_general(
        own, captions, (((1,), (1,)), ((), ())), preferred_element_type=jnp.float32
    )
    columns = jb * tc + lax.broadcasted_iota(jnp.int32, (1, tc), 1)
    own_weights = weights_of(own_scores, own_slot_ref[...] == columns)

    @pl.when(jb == 0)
    def _():
        image_out[...] = jnp.zeros_like(image_out)

    image_out[...] += scale * jnp.dot(own_weights, captions, preferred_element_type=jnp.float32)


def contrast_group(scale, shift, own_slot, slot_g, image_b_g, caption_b_g):
    group_rows, width = caption_b_g.shape
    rows = own_slot.shape[0]
    tc = 256
    return pl.pallas_call(
        contrast_kernel,
        grid=(group_rows // tc,),
        out_shape=(
            jax.ShapeDtypeStruct((group_rows, width), jnp.float32),
            jax.ShapeDtypeStruct((rows, width), jnp.float32),
        ),
        in_specs=[
            pl.BlockSpec(memory_space=pltpu.SMEM),
            pl.BlockSpec(memory_space=pltpu.SMEM),
            pl.BlockSpec((rows, 1), lambda j: (0, 0)),
            pl.BlockSpec((1, group_rows), lambda j: (0, 0)),
            pl.BlockSpec((group_rows, width), lambda j: (0, 0)),
            pl.BlockSpec((tc, width), lambda j: (j, 0)),
        ],
        out_specs=(
            pl.BlockSpec((tc, width), lambda j: (j, 0)),
            pl.BlockSpec((rows, width), lambda j: (0, 0)),
        ),
        compiler_params=pltpu.CompilerParams(dimension_semantics=("arbitrary",)),
        cost_estimate=pl.CostEstimate(
            flops=4 * group_rows * (group_rows + rows) * width,
            bytes_accessed=2 * group_rows * width * 2 + (group_rows + rows) * width * 4,
            transcendentals=group_rows * (group_rows + rows),
        ),
    )(scale, shift, own_slot.reshape((rows, 1)), slot_g.reshape((1, group_rows)), image_b_g, caption_b_g)


def unit_rows(values):
    return values * lax.rsqrt(jnp.sum(values * values, axis=1, keepdims=True) + 1e-06)


def text_embed(features, closing_layernorm_multiplier):
    center = features - jnp.mean(features, axis=1, keepdims=True)
    spread = jnp.mean(center * center, axis=1, keepdims=True)
    return unit_rows(center * lax.rsqrt(spread + 1e-05) * closing_layernorm_multiplier)


def sigmoid_weights(scores, labels):
    return (-labels * jax.nn.sigmoid(-labels * scores)).astype(jnp.bfloat16)


def shards(
    picture_embeds,
    matched_slot,
    summary_token_states,
    feedforward_inner_activations,
    closing_layernorm_multiplier,
    contracting_matrix,
    sharpness_factor,
    additive_shift_learned,
):
    similarity_multiplier = sharpness_factor[0]
    shift_value = additive_shift_learned[0]
    local_rows, width = picture_embeds.shape

    dp_size = lax.axis_size("dp")
    zero_size = lax.axis_size("zero")
    dp_place = lax.axis_index("dp")
    own_start = dp_place * local_rows
    transpose_route = [
        (a * zero_size + b, b * zero_size + a) for a in range(dp_size) for b in range(zero_size)
    ]

    ffa_cols = lax.all_to_all(
        feedforward_inner_activations, "dp", split_axis=1, concat_axis=0, tiled=True
    )
    weight_block = lax.ppermute(contracting_matrix, ("dp", "zero"), transpose_route)

    digits = jnp.zeros((local_rows, 128), jnp.bfloat16)
    digits = digits.at[:, 0].set((matched_slot // 256).astype(jnp.bfloat16))
    digits = digits.at[:, 1].set((matched_slot % 256).astype(jnp.bfloat16))
    both = jnp.concatenate([picture_embeds, summary_token_states, digits], axis=1)
    both_g = gather_dp(both).reshape((-1, both.shape[1]))
    ffa_cols, weight_block, both_g = lax.optimization_barrier((ffa_cols, weight_block, both_g))
    slot_g = both_g[:, 2 * width].astype(jnp.int32) * 256 + both_g[:, 2 * width + 1].astype(
        jnp.int32
    )
    image_b_g = unit_rows(both_g[:, :width].astype(jnp.float32)).astype(jnp.bfloat16)
    caption_g, caption_back = jax.vjp(
        lambda feats: text_embed(feats, closing_layernorm_multiplier),
        both_g[:, width : 2 * width].astype(jnp.float32),
    )
    caption_b_g = caption_g.astype(jnp.bfloat16)
    group_rows = caption_b_g.shape[0]

    unit_image, image_back = jax.vjp(unit_rows, picture_embeds.astype(jnp.float32))

    caption_term, image_term = contrast_group(
        sharpness_factor, additive_shift_learned, matched_slot, slot_g, image_b_g, caption_b_g
    )

    image_grad = image_back(image_term)[0]
    upstream_g = caption_back(caption_term)[0].astype(jnp.bfloat16)

    hidden_part = lax.dot_general(
        upstream_g,
        weight_block,
        (((1,), (1,)), ((), ())),
        preferred_element_type=jnp.float32,
    ).astype(jnp.bfloat16)
    hidden_grad = lax.all_to_all(hidden_part, "dp", split_axis=0, concat_axis=1, tiled=True)
    group_sum = lax.dot_general(
        ffa_cols, upstream_g, (((0,), (0,)), ((), ())), preferred_element_type=jnp.float32
    )
    down_parts = lax.all_to_all(group_sum, "zero", split_axis=1, concat_axis=0, tiled=True)
    down_block = jnp.sum(down_parts.reshape((zero_size,) + (group_sum.shape[0], -1)), axis=0)
    down_grad = lax.ppermute(down_block, ("dp", "zero"), transpose_route)
    return (image_grad, hidden_grad, down_grad)


def solution(mesh):
    placed = (
        P(("dp", "zero"), None),
        P(("dp", "zero")),
        P(("dp", "zero"), None),
        P(("dp", "zero"), None),
        P(),
        P("zero", None),
        P(),
        P(),
    )
    return jax.shard_map(
        shards,
        mesh=mesh,
        in_specs=placed,
        out_specs=(P(("dp", "zero"), None), P(("dp", "zero"), None), P("zero", "dp")),
        check_vma=False,
    )
```

```python
import functools

import jax
import jax.numpy as jnp
from jax import lax
from jax.experimental import pallas as pl
from jax.experimental.pallas import tpu as pltpu
from jax.sharding import PartitionSpec as P

MESH = pl.DeviceIdType.MESH


def gather_kernel(chips, block_ref, out_ref, send_sem, recv_sem, local_sem):
    me = lax.axis_index("dp")
    zz = lax.axis_index("zero")
    core = me % 2
    chip = me // 2
    sibling = me + 1 - 2 * core

    def peer(k):
        return ((chip + k) % chips) * 2 + core

    def source(k):
        return ((chip + chips - k) % chips) * 2 + core

    barrier = pltpu.get_barrier_semaphore()
    pl.semaphore_signal(barrier, inc=1, device_id=(sibling, zz), device_id_type=MESH)
    for k in range(1, chips):
        pl.semaphore_signal(barrier, inc=1, device_id=(peer(k), zz), device_id_type=MESH)
    pl.semaphore_wait(barrier, chips)

    local = pltpu.make_async_copy(block_ref, out_ref.at[me], local_sem)
    local.start()
    sends = []
    for k in range(1, chips):
        copy = pltpu.make_async_remote_copy(
            src_ref=block_ref,
            dst_ref=out_ref.at[me],
            send_sem=send_sem.at[k],
            recv_sem=recv_sem.at[me],
            device_id=(peer(k), zz),
            device_id_type=MESH,
        )
        copy.start()
        sends.append(copy)
    copy = pltpu.make_async_remote_copy(
        src_ref=block_ref,
        dst_ref=out_ref.at[me],
        send_sem=send_sem.at[0],
        recv_sem=recv_sem.at[me],
        device_id=(sibling, zz),
        device_id_type=MESH,
    )
    copy.start()
    sends.append(copy)
    for k in range(1, chips):
        s = source(k)
        arrived = pltpu.make_async_remote_copy(
            src_ref=out_ref.at[s],
            dst_ref=out_ref.at[s],
            send_sem=send_sem.at[chips + k],
            recv_sem=recv_sem.at[s],
            device_id=(sibling, zz),
            device_id_type=MESH,
        )
        arrived.wait_recv()
        arrived.start()
        sends.append(arrived)
    for k in range(chips):
        t = ((chip + k) % chips) * 2 + (1 - core)
        pltpu.make_async_remote_copy(
            src_ref=out_ref.at[t],
            dst_ref=out_ref.at[t],
            send_sem=send_sem.at[0],
            recv_sem=recv_sem.at[t],
            device_id=(sibling, zz),
            device_id_type=MESH,
        ).wait_recv()
    for copy in sends:
        copy.wait_send()
    local.wait()


def gather_dp(block):
    dp_size = lax.axis_size("dp")
    return pl.pallas_call(
        functools.partial(gather_kernel, dp_size // 2),
        out_shape=jax.ShapeDtypeStruct((dp_size,) + block.shape, block.dtype),
        in_specs=[pl.BlockSpec(memory_space=pl.ANY)],
        out_specs=pl.BlockSpec(memory_space=pl.ANY),
        scratch_shapes=[
            pltpu.SemaphoreType.DMA((dp_size,)),
            pltpu.SemaphoreType.DMA((dp_size,)),
            pltpu.SemaphoreType.DMA(()),
        ],
        compiler_params=pltpu.CompilerParams(collective_id=0, has_side_effects=True),
    )(block)


def contrast_kernel(
    scale_ref, shift_ref, own_slot_ref, slot_ref, images_ref, captions_ref,
    caption_out, image_out,
):
    jb = pl.program_id(0)
    tc = captions_ref.shape[0]
    rows = own_slot_ref.shape[0]
    scale = scale_ref[0]
    half_scale = 0.5 * scale
    half_shift = 0.5 * shift_ref[0]
    captions = captions_ref[...]
    places = jb * tc + lax.broadcasted_iota(jnp.int32, (tc, 1), 0)

    def weights_of(products, positive):
        half = 0.5 * jnp.tanh(half_scale * products + half_shift)
        return jnp.where(positive, half - 0.5, half + 0.5).astype(jnp.bfloat16)

    images = images_ref[...]
    products = lax.dot_general(
        captions, images, (((1,), (1,)), ((), ())), preferred_element_type=jnp.float32
    )
    weights = weights_of(products, slot_ref[...] == places)
    acc = jnp.dot(weights, images, preferred_element_type=jnp.float32)
    caption_out[...] = scale * acc

    own_start = pl.multiple_of(lax.axis_index("dp") * rows, rows)
    own = images_ref[pl.ds(own_start, rows), :]
    own_scores = lax.dot_general(
        own, captions, (((1,), (1,)), ((), ())), preferred_element_type=jnp.float32
    )
    columns = jb * tc + lax.broadcasted_iota(jnp.int32, (1, tc), 1)
    own_weights = weights_of(own_scores, own_slot_ref[...] == columns)

    @pl.when(jb == 0)
    def _():
        image_out[...] = jnp.zeros_like(image_out)

    image_out[...] += scale * jnp.dot(own_weights, captions, preferred_element_type=jnp.float32)


def contrast_group(scale, shift, own_slot, slot_g, image_b_g, caption_b_g):
    group_rows, width = caption_b_g.shape
    rows = own_slot.shape[0]
    tc = 512
    return pl.pallas_call(
        contrast_kernel,
        grid=(group_rows // tc,),
        out_shape=(
            jax.ShapeDtypeStruct((group_rows, width), jnp.float32),
            jax.ShapeDtypeStruct((rows, width), jnp.float32),
        ),
        in_specs=[
            pl.BlockSpec(memory_space=pltpu.SMEM),
            pl.BlockSpec(memory_space=pltpu.SMEM),
            pl.BlockSpec((rows, 1), lambda j: (0, 0)),
            pl.BlockSpec((1, group_rows), lambda j: (0, 0)),
            pl.BlockSpec((group_rows, width), lambda j: (0, 0)),
            pl.BlockSpec((tc, width), lambda j: (j, 0)),
        ],
        out_specs=(
            pl.BlockSpec((tc, width), lambda j: (j, 0)),
            pl.BlockSpec((rows, width), lambda j: (0, 0)),
        ),
        compiler_params=pltpu.CompilerParams(dimension_semantics=("arbitrary",)),
        cost_estimate=pl.CostEstimate(
            flops=4 * group_rows * (group_rows + rows) * width,
            bytes_accessed=2 * group_rows * width * 2 + (group_rows + rows) * width * 4,
            transcendentals=group_rows * (group_rows + rows),
        ),
    )(scale, shift, own_slot.reshape((rows, 1)), slot_g.reshape((1, group_rows)), image_b_g, caption_b_g)


def unit_rows(values):
    return values * lax.rsqrt(jnp.sum(values * values, axis=1, keepdims=True) + 1e-06)


def text_embed(features, closing_layernorm_multiplier):
    center = features - jnp.mean(features, axis=1, keepdims=True)
    spread = jnp.mean(center * center, axis=1, keepdims=True)
    return unit_rows(center * lax.rsqrt(spread + 1e-05) * closing_layernorm_multiplier)


def sigmoid_weights(scores, labels):
    return (-labels * jax.nn.sigmoid(-labels * scores)).astype(jnp.bfloat16)


def shards(
    picture_embeds,
    matched_slot,
    summary_token_states,
    feedforward_inner_activations,
    closing_layernorm_multiplier,
    contracting_matrix,
    sharpness_factor,
    additive_shift_learned,
):
    similarity_multiplier = sharpness_factor[0]
    shift_value = additive_shift_learned[0]
    local_rows, width = picture_embeds.shape

    dp_size = lax.axis_size("dp")
    zero_size = lax.axis_size("zero")
    dp_place = lax.axis_index("dp")
    own_start = dp_place * local_rows
    transpose_route = [
        (a * zero_size + b, b * zero_size + a) for a in range(dp_size) for b in range(zero_size)
    ]

    ffa_cols = lax.all_to_all(
        feedforward_inner_activations, "dp", split_axis=1, concat_axis=0, tiled=True
    )
    weight_block = lax.ppermute(contracting_matrix, ("dp", "zero"), transpose_route)

    digits = jnp.zeros((local_rows, 128), jnp.bfloat16)
    digits = digits.at[:, 0].set((matched_slot // 256).astype(jnp.bfloat16))
    digits = digits.at[:, 1].set((matched_slot % 256).astype(jnp.bfloat16))
    both = jnp.concatenate([picture_embeds, summary_token_states, digits], axis=1)
    both_g = gather_dp(both).reshape((-1, both.shape[1]))
    ffa_cols, weight_block, both_g = lax.optimization_barrier((ffa_cols, weight_block, both_g))
    slot_g = both_g[:, 2 * width].astype(jnp.int32) * 256 + both_g[:, 2 * width + 1].astype(
        jnp.int32
    )
    image_b_g = unit_rows(both_g[:, :width].astype(jnp.float32)).astype(jnp.bfloat16)
    caption_g, caption_back = jax.vjp(
        lambda feats: text_embed(feats, closing_layernorm_multiplier),
        both_g[:, width : 2 * width].astype(jnp.float32),
    )
    caption_b_g = caption_g.astype(jnp.bfloat16)
    group_rows = caption_b_g.shape[0]

    unit_image, image_back = jax.vjp(unit_rows, picture_embeds.astype(jnp.float32))

    caption_term, image_term = contrast_group(
        sharpness_factor, additive_shift_learned, matched_slot, slot_g, image_b_g, caption_b_g
    )

    image_grad = image_back(image_term)[0]
    upstream_g = caption_back(caption_term)[0].astype(jnp.bfloat16)

    hidden_part = lax.dot_general(
        upstream_g,
        weight_block,
        (((1,), (1,)), ((), ())),
        preferred_element_type=jnp.float32,
    ).astype(jnp.bfloat16)
    hidden_grad = lax.all_to_all(hidden_part, "dp", split_axis=0, concat_axis=1, tiled=True)
    group_sum = lax.dot_general(
        ffa_cols, upstream_g, (((0,), (0,)), ((), ())), preferred_element_type=jnp.float32
    )
    down_parts = lax.all_to_all(group_sum, "zero", split_axis=1, concat_axis=0, tiled=True)
    down_block = jnp.sum(down_parts.reshape((zero_size,) + (group_sum.shape[0], -1)), axis=0)
    down_grad = lax.ppermute(down_block, ("dp", "zero"), transpose_route)
    return (image_grad, hidden_grad, down_grad)


def solution(mesh):
    placed = (
        P(("dp", "zero"), None),
        P(("dp", "zero")),
        P(("dp", "zero"), None),
        P(("dp", "zero"), None),
        P(),
        P("zero", None),
        P(),
        P(),
    )
    return jax.shard_map(
        shards,
        mesh=mesh,
        in_specs=placed,
        out_specs=(P(("dp", "zero"), None), P(("dp", "zero"), None), P("zero", "dp")),
        check_vma=False,
    )
```

```python
import functools

import jax
import jax.numpy as jnp
from jax import lax
from jax.experimental import pallas as pl
from jax.experimental.pallas import tpu as pltpu
from jax.sharding import PartitionSpec as P

MESH = pl.DeviceIdType.MESH


def gather_kernel(chips, m, *refs):
    block_refs, out_refs = refs[:m], refs[m : 2 * m]
    send_sem, recv_sem, local_sem = refs[2 * m :]
    me = lax.axis_index("dp")
    zz = lax.axis_index("zero")
    core = me % 2
    chip = me // 2
    sibling = me + 1 - 2 * core

    def peer(k):
        return ((chip + k) % chips) * 2 + core

    def source(k):
        return ((chip + chips - k) % chips) * 2 + core

    barrier = pltpu.get_barrier_semaphore()
    pl.semaphore_signal(barrier, inc=1, device_id=(sibling, zz), device_id_type=MESH)
    for k in range(1, chips):
        pl.semaphore_signal(barrier, inc=1, device_id=(peer(k), zz), device_id_type=MESH)
    pl.semaphore_wait(barrier, chips)

    def remote(i, src, slot, send_index, target):
        return pltpu.make_async_remote_copy(
            src_ref=src,
            dst_ref=out_refs[i].at[slot],
            send_sem=send_sem.at[i, send_index],
            recv_sem=recv_sem.at[i, slot],
            device_id=(target, zz),
            device_id_type=MESH,
        )

    locals_ = []
    sends = []
    for i in range(m):
        local = pltpu.make_async_copy(block_refs[i], out_refs[i].at[me], local_sem.at[i])
        local.start()
        locals_.append(local)
    for k in range(1, chips):
        for i in range(m):
            copy = remote(i, block_refs[i], me, k, peer(k))
            copy.start()
            sends.append(copy)
    for i in range(m):
        copy = remote(i, block_refs[i], me, 0, sibling)
        copy.start()
        sends.append(copy)
    for k in range(1, chips):
        s = source(k)
        for i in range(m):
            arrived = remote(i, out_refs[i].at[s], s, chips + k, sibling)
            arrived.wait_recv()
            arrived.start()
            sends.append(arrived)
    for k in range(chips):
        t = ((chip + k) % chips) * 2 + (1 - core)
        for i in range(m):
            remote(i, out_refs[i].at[t], t, 0, sibling).wait_recv()
    for copy in sends:
        copy.wait_send()
    for local in locals_:
        local.wait()


def gather_dp(*blocks):
    dp_size = lax.axis_size("dp")
    m = len(blocks)
    return pl.pallas_call(
        functools.partial(gather_kernel, dp_size // 2, m),
        out_shape=tuple(
            jax.ShapeDtypeStruct((dp_size,) + block.shape, block.dtype) for block in blocks
        ),
        in_specs=[pl.BlockSpec(memory_space=pl.ANY)] * m,
        out_specs=tuple(pl.BlockSpec(memory_space=pl.ANY) for _ in blocks),
        scratch_shapes=[
            pltpu.SemaphoreType.DMA((m, dp_size)),
            pltpu.SemaphoreType.DMA((m, dp_size)),
            pltpu.SemaphoreType.DMA((m,)),
        ],
        compiler_params=pltpu.CompilerParams(collective_id=0, has_side_effects=True),
    )(*blocks)


def contrast_kernel(
    scale_ref, shift_ref, own_slot_ref, slot_ref, images_ref, captions_ref,
    caption_out, image_out,
):
    jb = pl.program_id(0)
    tc = captions_ref.shape[0]
    rows = own_slot_ref.shape[0]
    scale = scale_ref[0]
    half_scale = 0.5 * scale
    half_shift = 0.5 * shift_ref[0]
    captions = captions_ref[...]
    places = jb * tc + lax.broadcasted_iota(jnp.int32, (tc, 1), 0)

    def weights_of(products, positive):
        half = 0.5 * jnp.tanh(half_scale * products + half_shift)
        return jnp.where(positive, half - 0.5, half + 0.5).astype(jnp.bfloat16)

    images = images_ref[...]
    products = lax.dot_general(
        captions, images, (((1,), (1,)), ((), ())), preferred_element_type=jnp.float32
    )
    weights = weights_of(products, slot_ref[...] == places)
    acc = jnp.dot(weights, images, preferred_element_type=jnp.float32)
    caption_out[...] = scale * acc

    own_start = pl.multiple_of(lax.axis_index("dp") * rows, rows)
    own = images_ref[pl.ds(own_start, rows), :]
    own_scores = lax.dot_general(
        own, captions, (((1,), (1,)), ((), ())), preferred_element_type=jnp.float32
    )
    columns = jb * tc + lax.broadcasted_iota(jnp.int32, (1, tc), 1)
    own_weights = weights_of(own_scores, own_slot_ref[...] == columns)

    @pl.when(jb == 0)
    def _():
        image_out[...] = jnp.zeros_like(image_out)

    image_out[...] += scale * jnp.dot(own_weights, captions, preferred_element_type=jnp.float32)


def contrast_group(scale, shift, own_slot, slot_g, image_b_g, caption_b_g):
    group_rows, width = caption_b_g.shape
    rows = own_slot.shape[0]
    tc = 512
    return pl.pallas_call(
        contrast_kernel,
        grid=(group_rows // tc,),
        out_shape=(
            jax.ShapeDtypeStruct((group_rows, width), jnp.float32),
            jax.ShapeDtypeStruct((rows, width), jnp.float32),
        ),
        in_specs=[
            pl.BlockSpec(memory_space=pltpu.SMEM),
            pl.BlockSpec(memory_space=pltpu.SMEM),
            pl.BlockSpec((rows, 1), lambda j: (0, 0)),
            pl.BlockSpec((1, group_rows), lambda j: (0, 0)),
            pl.BlockSpec((group_rows, width), lambda j: (0, 0)),
            pl.BlockSpec((tc, width), lambda j: (j, 0)),
        ],
        out_specs=(
            pl.BlockSpec((tc, width), lambda j: (j, 0)),
            pl.BlockSpec((rows, width), lambda j: (0, 0)),
        ),
        compiler_params=pltpu.CompilerParams(dimension_semantics=("arbitrary",)),
        cost_estimate=pl.CostEstimate(
            flops=4 * group_rows * (group_rows + rows) * width,
            bytes_accessed=2 * group_rows * width * 2 + (group_rows + rows) * width * 4,
            transcendentals=group_rows * (group_rows + rows),
        ),
    )(scale, shift, own_slot.reshape((rows, 1)), slot_g.reshape((1, group_rows)), image_b_g, caption_b_g)


def unit_rows(values):
    return values * lax.rsqrt(jnp.sum(values * values, axis=1, keepdims=True) + 1e-06)


def text_embed(features, closing_layernorm_multiplier):
    center = features - jnp.mean(features, axis=1, keepdims=True)
    spread = jnp.mean(center * center, axis=1, keepdims=True)
    return unit_rows(center * lax.rsqrt(spread + 1e-05) * closing_layernorm_multiplier)


def sigmoid_weights(scores, labels):
    return (-labels * jax.nn.sigmoid(-labels * scores)).astype(jnp.bfloat16)


def shards(
    picture_embeds,
    matched_slot,
    summary_token_states,
    feedforward_inner_activations,
    closing_layernorm_multiplier,
    contracting_matrix,
    sharpness_factor,
    additive_shift_learned,
):
    similarity_multiplier = sharpness_factor[0]
    shift_value = additive_shift_learned[0]
    local_rows, width = picture_embeds.shape

    dp_size = lax.axis_size("dp")
    zero_size = lax.axis_size("zero")
    dp_place = lax.axis_index("dp")
    own_start = dp_place * local_rows
    transpose_route = [
        (a * zero_size + b, b * zero_size + a) for a in range(dp_size) for b in range(zero_size)
    ]

    ffa_cols = lax.all_to_all(
        feedforward_inner_activations, "dp", split_axis=1, concat_axis=0, tiled=True
    )
    weight_block = lax.ppermute(contracting_matrix, ("dp", "zero"), transpose_route)

    digits = jnp.zeros((16, local_rows), jnp.bfloat16)
    digits = digits.at[0].set((matched_slot // 256).astype(jnp.bfloat16))
    digits = digits.at[1].set((matched_slot % 256).astype(jnp.bfloat16))
    both = jnp.concatenate([picture_embeds, summary_token_states], axis=1)
    both_g, digits_g = gather_dp(both, digits)
    both_g = both_g.reshape((-1, both.shape[1]))
    ffa_cols, weight_block, both_g, digits_g = lax.optimization_barrier(
        (ffa_cols, weight_block, both_g, digits_g)
    )
    slot_g = (
        digits_g[:, 0, :].astype(jnp.int32) * 256 + digits_g[:, 1, :].astype(jnp.int32)
    ).reshape((-1,))
    image_b_g = unit_rows(both_g[:, :width].astype(jnp.float32)).astype(jnp.bfloat16)
    caption_g, caption_back = jax.vjp(
        lambda feats: text_embed(feats, closing_layernorm_multiplier),
        both_g[:, width : 2 * width].astype(jnp.float32),
    )
    caption_b_g = caption_g.astype(jnp.bfloat16)
    group_rows = caption_b_g.shape[0]

    unit_image, image_back = jax.vjp(unit_rows, picture_embeds.astype(jnp.float32))

    caption_term, image_term = contrast_group(
        sharpness_factor, additive_shift_learned, matched_slot, slot_g, image_b_g, caption_b_g
    )

    image_grad = image_back(image_term)[0]
    upstream_g = caption_back(caption_term)[0].astype(jnp.bfloat16)

    hidden_part = lax.dot_general(
        upstream_g,
        weight_block,
        (((1,), (1,)), ((), ())),
        preferred_element_type=jnp.float32,
    ).astype(jnp.bfloat16)
    hidden_grad = lax.all_to_all(hidden_part, "dp", split_axis=0, concat_axis=1, tiled=True)
    group_sum = lax.dot_general(
        ffa_cols, upstream_g, (((0,), (0,)), ((), ())), preferred_element_type=jnp.float32
    )
    down_parts = lax.all_to_all(group_sum, "zero", split_axis=1, concat_axis=0, tiled=True)
    down_block = jnp.sum(down_parts.reshape((zero_size,) + (group_sum.shape[0], -1)), axis=0)
    down_grad = lax.ppermute(down_block, ("dp", "zero"), transpose_route)
    return (image_grad, hidden_grad, down_grad)


def solution(mesh):
    placed = (
        P(("dp", "zero"), None),
        P(("dp", "zero")),
        P(("dp", "zero"), None),
        P(("dp", "zero"), None),
        P(),
        P("zero", None),
        P(),
        P(),
    )
    return jax.shard_map(
        shards,
        mesh=mesh,
        in_specs=placed,
        out_specs=(P(("dp", "zero"), None), P(("dp", "zero"), None), P("zero", "dp")),
        check_vma=False,
    )
```

```python
import functools

import jax
import jax.numpy as jnp
from jax import lax
from jax.experimental import pallas as pl
from jax.experimental.pallas import tpu as pltpu
from jax.sharding import PartitionSpec as P

MESH = pl.DeviceIdType.MESH


def gather_kernel(chips, m, *refs):
    block_refs, out_refs = refs[:m], refs[m : 2 * m]
    send_sem, recv_sem, local_sem = refs[2 * m :]
    me = lax.axis_index("dp")
    zz = lax.axis_index("zero")
    core = me % 2
    chip = me // 2
    sibling = me + 1 - 2 * core

    def peer(k):
        return ((chip + k) % chips) * 2 + core

    def source(k):
        return ((chip + chips - k) % chips) * 2 + core

    barrier = pltpu.get_barrier_semaphore()
    pl.semaphore_signal(barrier, inc=1, device_id=(sibling, zz), device_id_type=MESH)
    for k in range(1, chips):
        pl.semaphore_signal(barrier, inc=1, device_id=(peer(k), zz), device_id_type=MESH)
    pl.semaphore_wait(barrier, chips)

    def remote(i, src, slot, send_index, target):
        return pltpu.make_async_remote_copy(
            src_ref=src,
            dst_ref=out_refs[i].at[slot],
            send_sem=send_sem.at[i, send_index],
            recv_sem=recv_sem.at[i, slot],
            device_id=(target, zz),
            device_id_type=MESH,
        )

    locals_ = []
    sends = []
    for i in range(m):
        local = pltpu.make_async_copy(block_refs[i], out_refs[i].at[me], local_sem.at[i])
        local.start()
        locals_.append(local)
    for k in range(1, chips):
        for i in range(m):
            copy = remote(i, block_refs[i], me, k, peer(k))
            copy.start()
            sends.append(copy)
    for i in range(m):
        copy = remote(i, block_refs[i], me, 0, sibling)
        copy.start()
        sends.append(copy)
    for k in range(1, chips):
        s = source(k)
        for i in range(m):
            arrived = remote(i, out_refs[i].at[s], s, chips + k, sibling)
            arrived.wait_recv()
            arrived.start()
            sends.append(arrived)
    for k in range(chips):
        t = ((chip + k) % chips) * 2 + (1 - core)
        for i in range(m):
            remote(i, out_refs[i].at[t], t, 0, sibling).wait_recv()
    for copy in sends:
        copy.wait_send()
    for local in locals_:
        local.wait()


def gather_dp(*blocks):
    dp_size = lax.axis_size("dp")
    m = len(blocks)
    return pl.pallas_call(
        functools.partial(gather_kernel, dp_size // 2, m),
        out_shape=tuple(
            jax.ShapeDtypeStruct((dp_size,) + block.shape, block.dtype) for block in blocks
        ),
        in_specs=[pl.BlockSpec(memory_space=pl.ANY)] * m,
        out_specs=tuple(pl.BlockSpec(memory_space=pl.ANY) for _ in blocks),
        scratch_shapes=[
            pltpu.SemaphoreType.DMA((m, dp_size)),
            pltpu.SemaphoreType.DMA((m, dp_size)),
            pltpu.SemaphoreType.DMA((m,)),
        ],
        compiler_params=pltpu.CompilerParams(collective_id=0, has_side_effects=True),
    )(*blocks)


def contrast_kernel(
    scale_ref, shift_ref, own_slot_ref, slot_ref, images_ref, feats_ref, gain_ref,
    upstream_out, image_out,
):
    jb = pl.program_id(0)
    tc = feats_ref.shape[0]
    width = feats_ref.shape[1]
    rows = own_slot_ref.shape[0]
    scale = scale_ref[0]
    half_scale = 0.5 * scale
    half_shift = 0.5 * shift_ref[0]
    gain = gain_ref[...]

    feats = feats_ref[...].astype(jnp.float32)
    center = feats - jnp.sum(feats, axis=1, keepdims=True) / width
    spread = jnp.sum(center * center, axis=1, keepdims=True) / width
    inv_spread = lax.rsqrt(spread + 1e-05)
    normed = center * inv_spread * gain
    inv_norm = lax.rsqrt(jnp.sum(normed * normed, axis=1, keepdims=True) + 1e-06)
    captions = (normed * inv_norm).astype(jnp.bfloat16)
    places = jb * tc + lax.broadcasted_iota(jnp.int32, (tc, 1), 0)

    def weights_of(products, positive):
        half = 0.5 * jnp.tanh(half_scale * products + half_shift)
        return jnp.where(positive, half - 0.5, half + 0.5).astype(jnp.bfloat16)

    images = images_ref[...]
    products = lax.dot_general(
        captions, images, (((1,), (1,)), ((), ())), preferred_element_type=jnp.float32
    )
    weights = weights_of(products, slot_ref[...] == places)
    caption_grad = scale * jnp.dot(weights, images, preferred_element_type=jnp.float32)

    along = jnp.sum(caption_grad * normed, axis=1, keepdims=True)
    normed_grad = inv_norm * caption_grad - inv_norm * inv_norm * inv_norm * along * normed
    gained = gain * normed_grad
    spread_grad = -0.5 * inv_spread * inv_spread * inv_spread * jnp.sum(
        gained * center, axis=1, keepdims=True
    )
    center_grad = gained * inv_spread + (2.0 / width) * center * spread_grad
    feats_grad = center_grad - jnp.sum(center_grad, axis=1, keepdims=True) / width
    upstream_out[...] = feats_grad.astype(upstream_out.dtype)

    own_start = pl.multiple_of(lax.axis_index("dp") * rows, rows)
    own = images_ref[pl.ds(own_start, rows), :]
    own_scores = lax.dot_general(
        own, captions, (((1,), (1,)), ((), ())), preferred_element_type=jnp.float32
    )
    columns = jb * tc + lax.broadcasted_iota(jnp.int32, (1, tc), 1)
    own_weights = weights_of(own_scores, own_slot_ref[...] == columns)

    @pl.when(jb == 0)
    def _():
        image_out[...] = jnp.zeros_like(image_out)

    image_out[...] += scale * jnp.dot(own_weights, captions, preferred_element_type=jnp.float32)


def contrast_group(scale, shift, own_slot, slot_g, image_b_g, both_g, gain):
    group_rows, width = image_b_g.shape
    rows = own_slot.shape[0]
    tc = 512
    return pl.pallas_call(
        contrast_kernel,
        grid=(group_rows // tc,),
        out_shape=(
            jax.ShapeDtypeStruct((group_rows, width), jnp.bfloat16),
            jax.ShapeDtypeStruct((rows, width), jnp.float32),
        ),
        in_specs=[
            pl.BlockSpec(memory_space=pltpu.SMEM),
            pl.BlockSpec(memory_space=pltpu.SMEM),
            pl.BlockSpec((rows, 1), lambda j: (0, 0)),
            pl.BlockSpec((1, group_rows), lambda j: (0, 0)),
            pl.BlockSpec((group_rows, width), lambda j: (0, 0)),
            pl.BlockSpec((tc, width), lambda j: (j, 1)),
            pl.BlockSpec((1, width), lambda j: (0, 0)),
        ],
        out_specs=(
            pl.BlockSpec((tc, width), lambda j: (j, 0)),
            pl.BlockSpec((rows, width), lambda j: (0, 0)),
        ),
        compiler_params=pltpu.CompilerParams(dimension_semantics=("arbitrary",)),
        cost_estimate=pl.CostEstimate(
            flops=4 * group_rows * (group_rows + rows) * width,
            bytes_accessed=3 * group_rows * width * 2 + rows * width * 4,
            transcendentals=group_rows * (group_rows + rows),
        ),
    )(
        scale,
        shift,
        own_slot.reshape((rows, 1)),
        slot_g.reshape((1, group_rows)),
        image_b_g,
        both_g,
        gain.reshape((1, width)),
    )


def unit_rows(values):
    return values * lax.rsqrt(jnp.sum(values * values, axis=1, keepdims=True) + 1e-06)


def text_embed(features, closing_layernorm_multiplier):
    center = features - jnp.mean(features, axis=1, keepdims=True)
    spread = jnp.mean(center * center, axis=1, keepdims=True)
    return unit_rows(center * lax.rsqrt(spread + 1e-05) * closing_layernorm_multiplier)


def sigmoid_weights(scores, labels):
    return (-labels * jax.nn.sigmoid(-labels * scores)).astype(jnp.bfloat16)


def shards(
    picture_embeds,
    matched_slot,
    summary_token_states,
    feedforward_inner_activations,
    closing_layernorm_multiplier,
    contracting_matrix,
    sharpness_factor,
    additive_shift_learned,
):
    similarity_multiplier = sharpness_factor[0]
    shift_value = additive_shift_learned[0]
    local_rows, width = picture_embeds.shape

    dp_size = lax.axis_size("dp")
    zero_size = lax.axis_size("zero")
    dp_place = lax.axis_index("dp")
    own_start = dp_place * local_rows
    transpose_route = [
        (a * zero_size + b, b * zero_size + a) for a in range(dp_size) for b in range(zero_size)
    ]

    ffa_cols = lax.all_to_all(
        feedforward_inner_activations, "dp", split_axis=1, concat_axis=0, tiled=True
    )
    weight_block = lax.ppermute(contracting_matrix, ("dp", "zero"), transpose_route)

    digits = jnp.zeros((16, local_rows), jnp.bfloat16)
    digits = digits.at[0].set((matched_slot // 256).astype(jnp.bfloat16))
    digits = digits.at[1].set((matched_slot % 256).astype(jnp.bfloat16))
    both = jnp.concatenate([picture_embeds, summary_token_states], axis=1)
    both_g, digits_g = gather_dp(both, digits)
    both_g = both_g.reshape((-1, both.shape[1]))
    ffa_cols, weight_block, both_g, digits_g = lax.optimization_barrier(
        (ffa_cols, weight_block, both_g, digits_g)
    )
    slot_g = (
        digits_g[:, 0, :].astype(jnp.int32) * 256 + digits_g[:, 1, :].astype(jnp.int32)
    ).reshape((-1,))
    image_b_g = unit_rows(both_g[:, :width].astype(jnp.float32)).astype(jnp.bfloat16)

    unit_image, image_back = jax.vjp(unit_rows, picture_embeds.astype(jnp.float32))

    upstream_g, image_term = contrast_group(
        sharpness_factor,
        additive_shift_learned,
        matched_slot,
        slot_g,
        image_b_g,
        both_g,
        closing_layernorm_multiplier,
    )

    image_grad = image_back(image_term)[0]

    hidden_part = lax.dot_general(
        upstream_g,
        weight_block,
        (((1,), (1,)), ((), ())),
        preferred_element_type=jnp.float32,
    ).astype(jnp.bfloat16)
    hidden_grad = lax.all_to_all(hidden_part, "dp", split_axis=0, concat_axis=1, tiled=True)
    group_sum = lax.dot_general(
        ffa_cols, upstream_g, (((0,), (0,)), ((), ())), preferred_element_type=jnp.float32
    )
    down_parts = lax.all_to_all(group_sum, "zero", split_axis=1, concat_axis=0, tiled=True)
    down_block = jnp.sum(down_parts.reshape((zero_size,) + (group_sum.shape[0], -1)), axis=0)
    down_grad = lax.ppermute(down_block, ("dp", "zero"), transpose_route)
    return (image_grad, hidden_grad, down_grad)


def solution(mesh):
    placed = (
        P(("dp", "zero"), None),
        P(("dp", "zero")),
        P(("dp", "zero"), None),
        P(("dp", "zero"), None),
        P(),
        P("zero", None),
        P(),
        P(),
    )
    return jax.shard_map(
        shards,
        mesh=mesh,
        in_specs=placed,
        out_specs=(P(("dp", "zero"), None), P(("dp", "zero"), None), P("zero", "dp")),
        check_vma=False,
    )
```

```python
import functools

import jax
import jax.numpy as jnp
from jax import lax
from jax.experimental import pallas as pl
from jax.experimental.pallas import tpu as pltpu
from jax.sharding import PartitionSpec as P

MESH = pl.DeviceIdType.MESH


def gather_kernel(chips, m, *refs):
    block_refs, out_refs = refs[:m], refs[m : 2 * m]
    send_sem, recv_sem, local_sem = refs[2 * m :]
    me = lax.axis_index("dp")
    zz = lax.axis_index("zero")
    core = me % 2
    chip = me // 2
    sibling = me + 1 - 2 * core

    def peer(k):
        return ((chip + k) % chips) * 2 + core

    def source(k):
        return ((chip + chips - k) % chips) * 2 + core

    barrier = pltpu.get_barrier_semaphore()
    pl.semaphore_signal(barrier, inc=1, device_id=(sibling, zz), device_id_type=MESH)
    for k in range(1, chips):
        pl.semaphore_signal(barrier, inc=1, device_id=(peer(k), zz), device_id_type=MESH)
    pl.semaphore_wait(barrier, chips)

    def remote(i, src, slot, send_index, target):
        return pltpu.make_async_remote_copy(
            src_ref=src,
            dst_ref=out_refs[i].at[slot],
            send_sem=send_sem.at[i, send_index],
            recv_sem=recv_sem.at[i, slot],
            device_id=(target, zz),
            device_id_type=MESH,
        )

    locals_ = []
    sends = []
    for i in range(m):
        local = pltpu.make_async_copy(block_refs[i], out_refs[i].at[me], local_sem.at[i])
        local.start()
        locals_.append(local)
    for k in range(1, chips):
        for i in range(m):
            copy = remote(i, block_refs[i], me, k, peer(k))
            copy.start()
            sends.append(copy)
    for i in range(m):
        copy = remote(i, block_refs[i], me, 0, sibling)
        copy.start()
        sends.append(copy)
    for k in range(1, chips):
        s = source(k)
        for i in range(m):
            arrived = remote(i, out_refs[i].at[s], s, chips + k, sibling)
            arrived.wait_recv()
            arrived.start()
            sends.append(arrived)
    for k in range(chips):
        t = ((chip + k) % chips) * 2 + (1 - core)
        for i in range(m):
            remote(i, out_refs[i].at[t], t, 0, sibling).wait_recv()
    for copy in sends:
        copy.wait_send()
    for local in locals_:
        local.wait()


def gather_dp(*blocks):
    dp_size = lax.axis_size("dp")
    m = len(blocks)
    return pl.pallas_call(
        functools.partial(gather_kernel, dp_size // 2, m),
        out_shape=tuple(
            jax.ShapeDtypeStruct((dp_size,) + block.shape, block.dtype) for block in blocks
        ),
        in_specs=[pl.BlockSpec(memory_space=pl.ANY)] * m,
        out_specs=tuple(pl.BlockSpec(memory_space=pl.ANY) for _ in blocks),
        scratch_shapes=[
            pltpu.SemaphoreType.DMA((m, dp_size)),
            pltpu.SemaphoreType.DMA((m, dp_size)),
            pltpu.SemaphoreType.DMA((m,)),
        ],
        compiler_params=pltpu.CompilerParams(collective_id=0, has_side_effects=True),
    )(*blocks)


def contrast_kernel(
    scale_ref, shift_ref, own_slot_ref, slot_ref, raw_images_ref, feats_ref, gain_ref,
    upstream_out, image_out, images_ref,
):
    jb = pl.program_id(0)
    tc = feats_ref.shape[0]
    width = feats_ref.shape[1]
    rows = own_slot_ref.shape[0]
    scale = scale_ref[0]
    half_scale = 0.5 * scale
    half_shift = 0.5 * shift_ref[0]
    gain = gain_ref[...]

    feats = feats_ref[...].astype(jnp.float32)
    center = feats - jnp.sum(feats, axis=1, keepdims=True) / width
    spread = jnp.sum(center * center, axis=1, keepdims=True) / width
    inv_spread = lax.rsqrt(spread + 1e-05)
    normed = center * inv_spread * gain
    inv_norm = lax.rsqrt(jnp.sum(normed * normed, axis=1, keepdims=True) + 1e-06)
    captions = (normed * inv_norm).astype(jnp.bfloat16)
    places = jb * tc + lax.broadcasted_iota(jnp.int32, (tc, 1), 0)

    def weights_of(products, positive):
        half = 0.5 * jnp.tanh(half_scale * products + half_shift)
        return jnp.where(positive, half - 0.5, half + 0.5).astype(jnp.bfloat16)

    @pl.when(jb == 0)
    def _():
        def unit_chunk(c, carry):
            at = pl.ds(pl.multiple_of(c * tc, tc), tc)
            raw = raw_images_ref[at, :].astype(jnp.float32)
            images_ref[at, :] = (
                raw * lax.rsqrt(jnp.sum(raw * raw, axis=1, keepdims=True) + 1e-06)
            ).astype(images_ref.dtype)
            return carry

        lax.fori_loop(0, images_ref.shape[0] // tc, unit_chunk, 0)

    images = images_ref[...]
    products = lax.dot_general(
        captions, images, (((1,), (1,)), ((), ())), preferred_element_type=jnp.float32
    )
    weights = weights_of(products, slot_ref[...] == places)
    caption_grad = scale * jnp.dot(weights, images, preferred_element_type=jnp.float32)

    along = jnp.sum(caption_grad * normed, axis=1, keepdims=True)
    normed_grad = inv_norm * caption_grad - inv_norm * inv_norm * inv_norm * along * normed
    gained = gain * normed_grad
    spread_grad = -0.5 * inv_spread * inv_spread * inv_spread * jnp.sum(
        gained * center, axis=1, keepdims=True
    )
    center_grad = gained * inv_spread + (2.0 / width) * center * spread_grad
    feats_grad = center_grad - jnp.sum(center_grad, axis=1, keepdims=True) / width
    upstream_out[...] = feats_grad.astype(upstream_out.dtype)

    own_start = pl.multiple_of(lax.axis_index("dp") * rows, rows)
    own = images_ref[pl.ds(own_start, rows), :]
    own_scores = lax.dot_general(
        own, captions, (((1,), (1,)), ((), ())), preferred_element_type=jnp.float32
    )
    columns = jb * tc + lax.broadcasted_iota(jnp.int32, (1, tc), 1)
    own_weights = weights_of(own_scores, own_slot_ref[...] == columns)

    @pl.when(jb == 0)
    def _():
        image_out[...] = jnp.zeros_like(image_out)

    image_out[...] += scale * jnp.dot(own_weights, captions, preferred_element_type=jnp.float32)


def contrast_group(scale, shift, own_slot, slot_g, both_g, gain):
    group_rows, width = both_g.shape[0], gain.shape[0]
    rows = own_slot.shape[0]
    tc = 512
    return pl.pallas_call(
        contrast_kernel,
        grid=(group_rows // tc,),
        out_shape=(
            jax.ShapeDtypeStruct((group_rows, width), jnp.bfloat16),
            jax.ShapeDtypeStruct((rows, width), jnp.float32),
        ),
        in_specs=[
            pl.BlockSpec(memory_space=pltpu.SMEM),
            pl.BlockSpec(memory_space=pltpu.SMEM),
            pl.BlockSpec((rows, 1), lambda j: (0, 0)),
            pl.BlockSpec((1, group_rows), lambda j: (0, 0)),
            pl.BlockSpec((group_rows, width), lambda j: (0, 0)),
            pl.BlockSpec((tc, width), lambda j: (j, 1)),
            pl.BlockSpec((1, width), lambda j: (0, 0)),
        ],
        out_specs=(
            pl.BlockSpec((tc, width), lambda j: (j, 0)),
            pl.BlockSpec((rows, width), lambda j: (0, 0)),
        ),
        scratch_shapes=[pltpu.VMEM((group_rows, width), jnp.bfloat16)],
        compiler_params=pltpu.CompilerParams(dimension_semantics=("arbitrary",)),
        cost_estimate=pl.CostEstimate(
            flops=4 * group_rows * (group_rows + rows) * width,
            bytes_accessed=3 * group_rows * width * 2 + rows * width * 4,
            transcendentals=group_rows * (group_rows + rows),
        ),
    )(
        scale,
        shift,
        own_slot.reshape((rows, 1)),
        slot_g.reshape((1, group_rows)),
        both_g,
        both_g,
        gain.reshape((1, width)),
    )


def unit_rows(values):
    return values * lax.rsqrt(jnp.sum(values * values, axis=1, keepdims=True) + 1e-06)


def text_embed(features, closing_layernorm_multiplier):
    center = features - jnp.mean(features, axis=1, keepdims=True)
    spread = jnp.mean(center * center, axis=1, keepdims=True)
    return unit_rows(center * lax.rsqrt(spread + 1e-05) * closing_layernorm_multiplier)


def sigmoid_weights(scores, labels):
    return (-labels * jax.nn.sigmoid(-labels * scores)).astype(jnp.bfloat16)


def shards(
    picture_embeds,
    matched_slot,
    summary_token_states,
    feedforward_inner_activations,
    closing_layernorm_multiplier,
    contracting_matrix,
    sharpness_factor,
    additive_shift_learned,
):
    similarity_multiplier = sharpness_factor[0]
    shift_value = additive_shift_learned[0]
    local_rows, width = picture_embeds.shape

    dp_size = lax.axis_size("dp")
    zero_size = lax.axis_size("zero")
    dp_place = lax.axis_index("dp")
    own_start = dp_place * local_rows
    transpose_route = [
        (a * zero_size + b, b * zero_size + a) for a in range(dp_size) for b in range(zero_size)
    ]

    ffa_cols = lax.all_to_all(
        feedforward_inner_activations, "dp", split_axis=1, concat_axis=0, tiled=True
    )
    weight_block = lax.ppermute(contracting_matrix, ("dp", "zero"), transpose_route)

    digits = jnp.zeros((16, local_rows), jnp.bfloat16)
    digits = digits.at[0].set((matched_slot // 256).astype(jnp.bfloat16))
    digits = digits.at[1].set((matched_slot % 256).astype(jnp.bfloat16))
    both = jnp.concatenate([picture_embeds, summary_token_states], axis=1)
    both_g, digits_g = gather_dp(both, digits)
    both_g = both_g.reshape((-1, both.shape[1]))
    ffa_cols, weight_block, both_g, digits_g = lax.optimization_barrier(
        (ffa_cols, weight_block, both_g, digits_g)
    )
    slot_g = (
        digits_g[:, 0, :].astype(jnp.int32) * 256 + digits_g[:, 1, :].astype(jnp.int32)
    ).reshape((-1,))
    unit_image, image_back = jax.vjp(unit_rows, picture_embeds.astype(jnp.float32))

    upstream_g, image_term = contrast_group(
        sharpness_factor,
        additive_shift_learned,
        matched_slot,
        slot_g,
        both_g,
        closing_layernorm_multiplier,
    )

    image_grad = image_back(image_term)[0]

    hidden_part = lax.dot_general(
        upstream_g,
        weight_block,
        (((1,), (1,)), ((), ())),
        preferred_element_type=jnp.float32,
    ).astype(jnp.bfloat16)
    hidden_grad = lax.all_to_all(hidden_part, "dp", split_axis=0, concat_axis=1, tiled=True)
    group_sum = lax.dot_general(
        ffa_cols, upstream_g, (((0,), (0,)), ((), ())), preferred_element_type=jnp.float32
    )
    down_parts = lax.all_to_all(group_sum, "zero", split_axis=1, concat_axis=0, tiled=True)
    down_block = jnp.sum(down_parts.reshape((zero_size,) + (group_sum.shape[0], -1)), axis=0)
    down_grad = lax.ppermute(down_block, ("dp", "zero"), transpose_route)
    return (image_grad, hidden_grad, down_grad)


def solution(mesh):
    placed = (
        P(("dp", "zero"), None),
        P(("dp", "zero")),
        P(("dp", "zero"), None),
        P(("dp", "zero"), None),
        P(),
        P("zero", None),
        P(),
        P(),
    )
    return jax.shard_map(
        shards,
        mesh=mesh,
        in_specs=placed,
        out_specs=(P(("dp", "zero"), None), P(("dp", "zero"), None), P("zero", "dp")),
        check_vma=False,
    )
```

```python
import functools

import jax
import jax.numpy as jnp
from jax import lax
from jax.experimental import pallas as pl
from jax.experimental.pallas import tpu as pltpu
from jax.sharding import PartitionSpec as P

MESH = pl.DeviceIdType.MESH


def gather_kernel(chips, m, *refs):
    block_refs, out_refs = refs[:m], refs[m : 2 * m]
    send_sem, recv_sem, local_sem = refs[2 * m :]
    me = lax.axis_index("dp")
    zz = lax.axis_index("zero")
    core = me % 2
    chip = me // 2
    sibling = me + 1 - 2 * core

    def peer(k):
        return ((chip + k) % chips) * 2 + core

    def source(k):
        return ((chip + chips - k) % chips) * 2 + core

    barrier = pltpu.get_barrier_semaphore()
    pl.semaphore_signal(barrier, inc=1, device_id=(sibling, zz), device_id_type=MESH)
    for k in range(1, chips):
        pl.semaphore_signal(barrier, inc=1, device_id=(peer(k), zz), device_id_type=MESH)
    pl.semaphore_wait(barrier, chips)

    def remote(i, src, slot, send_index, target):
        return pltpu.make_async_remote_copy(
            src_ref=src,
            dst_ref=out_refs[i].at[slot],
            send_sem=send_sem.at[i, send_index],
            recv_sem=recv_sem.at[i, slot],
            device_id=(target, zz),
            device_id_type=MESH,
        )

    locals_ = []
    sends = []
    for i in range(m):
        local = pltpu.make_async_copy(block_refs[i], out_refs[i].at[me], local_sem.at[i])
        local.start()
        locals_.append(local)
    for k in range(1, chips):
        for i in range(m):
            copy = remote(i, block_refs[i], me, k, peer(k))
            copy.start()
            sends.append(copy)
    for i in range(m):
        copy = remote(i, block_refs[i], me, 0, sibling)
        copy.start()
        sends.append(copy)
    for k in range(1, chips):
        s = source(k)
        for i in range(m):
            arrived = remote(i, out_refs[i].at[s], s, chips + k, sibling)
            arrived.wait_recv()
            arrived.start()
            sends.append(arrived)
    for k in range(chips):
        t = ((chip + k) % chips) * 2 + (1 - core)
        for i in range(m):
            remote(i, out_refs[i].at[t], t, 0, sibling).wait_recv()
    for copy in sends:
        copy.wait_send()
    for local in locals_:
        local.wait()


def gather_dp(*blocks):
    dp_size = lax.axis_size("dp")
    m = len(blocks)
    return pl.pallas_call(
        functools.partial(gather_kernel, dp_size // 2, m),
        out_shape=tuple(
            jax.ShapeDtypeStruct((dp_size,) + block.shape, block.dtype) for block in blocks
        ),
        in_specs=[pl.BlockSpec(memory_space=pl.ANY)] * m,
        out_specs=tuple(pl.BlockSpec(memory_space=pl.ANY) for _ in blocks),
        scratch_shapes=[
            pltpu.SemaphoreType.DMA((m, dp_size)),
            pltpu.SemaphoreType.DMA((m, dp_size)),
            pltpu.SemaphoreType.DMA((m,)),
        ],
        compiler_params=pltpu.CompilerParams(collective_id=0, has_side_effects=True),
    )(*blocks)


def contrast_kernel(
    scale_ref, shift_ref, own_slot_ref, slot_ref, raw_images_ref, feats_ref, gain_ref,
    ffa_ref, weight_ref, hidden_out, sum_out, image_out, images_ref,
):
    jb = pl.program_id(0)
    tc = feats_ref.shape[0]
    width = feats_ref.shape[1]
    rows = own_slot_ref.shape[0]
    scale = scale_ref[0]
    half_scale = 0.5 * scale
    half_shift = 0.5 * shift_ref[0]
    gain = gain_ref[...]

    feats = feats_ref[...].astype(jnp.float32)
    center = feats - jnp.sum(feats, axis=1, keepdims=True) / width
    spread = jnp.sum(center * center, axis=1, keepdims=True) / width
    inv_spread = lax.rsqrt(spread + 1e-05)
    normed = center * inv_spread * gain
    inv_norm = lax.rsqrt(jnp.sum(normed * normed, axis=1, keepdims=True) + 1e-06)
    captions = (normed * inv_norm).astype(jnp.bfloat16)
    places = jb * tc + lax.broadcasted_iota(jnp.int32, (tc, 1), 0)

    def weights_of(products, positive):
        half = 0.5 * jnp.tanh(half_scale * products + half_shift)
        return jnp.where(positive, half - 0.5, half + 0.5).astype(jnp.bfloat16)

    @pl.when(jb == 0)
    def _():
        def unit_chunk(c, carry):
            at = pl.ds(pl.multiple_of(c * tc, tc), tc)
            raw = raw_images_ref[at, :].astype(jnp.float32)
            images_ref[at, :] = (
                raw * lax.rsqrt(jnp.sum(raw * raw, axis=1, keepdims=True) + 1e-06)
            ).astype(images_ref.dtype)
            return carry

        lax.fori_loop(0, images_ref.shape[0] // tc, unit_chunk, 0)

    images = images_ref[...]
    products = lax.dot_general(
        captions, images, (((1,), (1,)), ((), ())), preferred_element_type=jnp.float32
    )
    weights = weights_of(products, slot_ref[...] == places)
    caption_grad = scale * jnp.dot(weights, images, preferred_element_type=jnp.float32)

    along = jnp.sum(caption_grad * normed, axis=1, keepdims=True)
    normed_grad = inv_norm * caption_grad - inv_norm * inv_norm * inv_norm * along * normed
    gained = gain * normed_grad
    spread_grad = -0.5 * inv_spread * inv_spread * inv_spread * jnp.sum(
        gained * center, axis=1, keepdims=True
    )
    center_grad = gained * inv_spread + (2.0 / width) * center * spread_grad
    feats_grad = center_grad - jnp.sum(center_grad, axis=1, keepdims=True) / width
    upstream = feats_grad.astype(jnp.bfloat16)
    hidden_out[...] = lax.dot_general(
        upstream, weight_ref[...], (((1,), (1,)), ((), ())), preferred_element_type=jnp.float32
    ).astype(hidden_out.dtype)
    block_sum = lax.dot_general(
        ffa_ref[...], upstream, (((0,), (0,)), ((), ())), preferred_element_type=jnp.float32
    )

    @pl.when(jb == 0)
    def _():
        sum_out[...] = block_sum

    @pl.when(jb > 0)
    def _():
        sum_out[...] += block_sum

    own_start = pl.multiple_of(lax.axis_index("dp") * rows, rows)
    own = images_ref[pl.ds(own_start, rows), :]
    own_scores = lax.dot_general(
        own, captions, (((1,), (1,)), ((), ())), preferred_element_type=jnp.float32
    )
    columns = jb * tc + lax.broadcasted_iota(jnp.int32, (1, tc), 1)
    own_weights = weights_of(own_scores, own_slot_ref[...] == columns)

    @pl.when(jb == 0)
    def _():
        image_out[...] = jnp.zeros_like(image_out)

    image_out[...] += scale * jnp.dot(own_weights, captions, preferred_element_type=jnp.float32)


def contrast_group(scale, shift, own_slot, slot_g, both_g, gain, ffa_cols, weight_block):
    group_rows, width = both_g.shape[0], gain.shape[0]
    block_cols = weight_block.shape[0]
    rows = own_slot.shape[0]
    tc = 512
    return pl.pallas_call(
        contrast_kernel,
        grid=(group_rows // tc,),
        out_shape=(
            jax.ShapeDtypeStruct((group_rows, block_cols), jnp.bfloat16),
            jax.ShapeDtypeStruct((block_cols, width), jnp.float32),
            jax.ShapeDtypeStruct((rows, width), jnp.float32),
        ),
        in_specs=[
            pl.BlockSpec(memory_space=pltpu.SMEM),
            pl.BlockSpec(memory_space=pltpu.SMEM),
            pl.BlockSpec((rows, 1), lambda j: (0, 0)),
            pl.BlockSpec((1, group_rows), lambda j: (0, 0)),
            pl.BlockSpec((group_rows, width), lambda j: (0, 0)),
            pl.BlockSpec((tc, width), lambda j: (j, 1)),
            pl.BlockSpec((1, width), lambda j: (0, 0)),
            pl.BlockSpec((tc, block_cols), lambda j: (j, 0)),
            pl.BlockSpec((block_cols, width), lambda j: (0, 0)),
        ],
        out_specs=(
            pl.BlockSpec((tc, block_cols), lambda j: (j, 0)),
            pl.BlockSpec((block_cols, width), lambda j: (0, 0)),
            pl.BlockSpec((rows, width), lambda j: (0, 0)),
        ),
        scratch_shapes=[pltpu.VMEM((group_rows, width), jnp.bfloat16)],
        compiler_params=pltpu.CompilerParams(dimension_semantics=("arbitrary",)),
        cost_estimate=pl.CostEstimate(
            flops=4 * group_rows * (group_rows + rows) * width,
            bytes_accessed=3 * group_rows * width * 2 + rows * width * 4,
            transcendentals=group_rows * (group_rows + rows),
        ),
    )(
        scale,
        shift,
        own_slot.reshape((rows, 1)),
        slot_g.reshape((1, group_rows)),
        both_g,
        both_g,
        gain.reshape((1, width)),
        ffa_cols,
        weight_block,
    )


def unit_rows(values):
    return values * lax.rsqrt(jnp.sum(values * values, axis=1, keepdims=True) + 1e-06)


def text_embed(features, closing_layernorm_multiplier):
    center = features - jnp.mean(features, axis=1, keepdims=True)
    spread = jnp.mean(center * center, axis=1, keepdims=True)
    return unit_rows(center * lax.rsqrt(spread + 1e-05) * closing_layernorm_multiplier)


def sigmoid_weights(scores, labels):
    return (-labels * jax.nn.sigmoid(-labels * scores)).astype(jnp.bfloat16)


def shards(
    picture_embeds,
    matched_slot,
    summary_token_states,
    feedforward_inner_activations,
    closing_layernorm_multiplier,
    contracting_matrix,
    sharpness_factor,
    additive_shift_learned,
):
    similarity_multiplier = sharpness_factor[0]
    shift_value = additive_shift_learned[0]
    local_rows, width = picture_embeds.shape

    dp_size = lax.axis_size("dp")
    zero_size = lax.axis_size("zero")
    dp_place = lax.axis_index("dp")
    own_start = dp_place * local_rows
    transpose_route = [
        (a * zero_size + b, b * zero_size + a) for a in range(dp_size) for b in range(zero_size)
    ]

    ffa_cols = lax.all_to_all(
        feedforward_inner_activations, "dp", split_axis=1, concat_axis=0, tiled=True
    )
    weight_block = lax.ppermute(contracting_matrix, ("dp", "zero"), transpose_route)

    digits = jnp.zeros((16, local_rows), jnp.bfloat16)
    digits = digits.at[0].set((matched_slot // 256).astype(jnp.bfloat16))
    digits = digits.at[1].set((matched_slot % 256).astype(jnp.bfloat16))
    both = jnp.concatenate([picture_embeds, summary_token_states], axis=1)
    both_g, digits_g = gather_dp(both, digits)
    both_g = both_g.reshape((-1, both.shape[1]))
    ffa_cols, weight_block, both_g, digits_g = lax.optimization_barrier(
        (ffa_cols, weight_block, both_g, digits_g)
    )
    slot_g = (
        digits_g[:, 0, :].astype(jnp.int32) * 256 + digits_g[:, 1, :].astype(jnp.int32)
    ).reshape((-1,))
    unit_image, image_back = jax.vjp(unit_rows, picture_embeds.astype(jnp.float32))

    hidden_part, group_sum, image_term = contrast_group(
        sharpness_factor,
        additive_shift_learned,
        matched_slot,
        slot_g,
        both_g,
        closing_layernorm_multiplier,
        ffa_cols,
        weight_block,
    )

    image_grad = image_back(image_term)[0]

    hidden_grad = lax.all_to_all(hidden_part, "dp", split_axis=0, concat_axis=1, tiled=True)
    down_parts = lax.all_to_all(group_sum, "zero", split_axis=1, concat_axis=0, tiled=True)
    down_block = jnp.sum(down_parts.reshape((zero_size,) + (group_sum.shape[0], -1)), axis=0)
    down_grad = lax.ppermute(down_block, ("dp", "zero"), transpose_route)
    return (image_grad, hidden_grad, down_grad)


def solution(mesh):
    placed = (
        P(("dp", "zero"), None),
        P(("dp", "zero")),
        P(("dp", "zero"), None),
        P(("dp", "zero"), None),
        P(),
        P("zero", None),
        P(),
        P(),
    )
    return jax.shard_map(
        shards,
        mesh=mesh,
        in_specs=placed,
        out_specs=(P(("dp", "zero"), None), P(("dp", "zero"), None), P("zero", "dp")),
        check_vma=False,
    )
```

```python
import functools

import jax
import jax.numpy as jnp
from jax import lax
from jax.experimental import pallas as pl
from jax.experimental.pallas import tpu as pltpu
from jax.sharding import PartitionSpec as P

MESH = pl.DeviceIdType.MESH


def gather_kernel(chips, m, *refs):
    block_refs, out_refs = refs[:m], refs[m : 2 * m]
    send_sem, recv_sem, local_sem = refs[2 * m :]
    me = lax.axis_index("dp")
    zz = lax.axis_index("zero")
    core = me % 2
    chip = me // 2
    sibling = me + 1 - 2 * core

    def peer(k):
        return ((chip + k) % chips) * 2 + core

    def source(k):
        return ((chip + chips - k) % chips) * 2 + core

    barrier = pltpu.get_barrier_semaphore()
    pl.semaphore_signal(barrier, inc=1, device_id=(sibling, zz), device_id_type=MESH)
    for k in range(1, chips):
        pl.semaphore_signal(barrier, inc=1, device_id=(peer(k), zz), device_id_type=MESH)
    pl.semaphore_wait(barrier, chips)

    def remote(i, src, slot, send_index, target):
        return pltpu.make_async_remote_copy(
            src_ref=src,
            dst_ref=out_refs[i].at[slot],
            send_sem=send_sem.at[i, send_index],
            recv_sem=recv_sem.at[i, slot],
            device_id=(target, zz),
            device_id_type=MESH,
        )

    locals_ = []
    sends = []
    for i in range(m):
        local = pltpu.make_async_copy(block_refs[i], out_refs[i].at[me], local_sem.at[i])
        local.start()
        locals_.append(local)
    for k in range(1, chips):
        for i in range(m):
            copy = remote(i, block_refs[i], me, k, peer(k))
            copy.start()
            sends.append(copy)
    for i in range(m):
        copy = remote(i, block_refs[i], me, 0, sibling)
        copy.start()
        sends.append(copy)
    for k in range(1, chips):
        s = source(k)
        for i in range(m):
            arrived = remote(i, out_refs[i].at[s], s, chips + k, sibling)
            arrived.wait_recv()
            arrived.start()
            sends.append(arrived)
    for k in range(chips):
        t = ((chip + k) % chips) * 2 + (1 - core)
        for i in range(m):
            remote(i, out_refs[i].at[t], t, 0, sibling).wait_recv()
    for copy in sends:
        copy.wait_send()
    for local in locals_:
        local.wait()


def gather_dp(*blocks):
    dp_size = lax.axis_size("dp")
    m = len(blocks)
    return pl.pallas_call(
        functools.partial(gather_kernel, dp_size // 2, m),
        out_shape=tuple(
            jax.ShapeDtypeStruct((dp_size,) + block.shape, block.dtype) for block in blocks
        ),
        in_specs=[pl.BlockSpec(memory_space=pl.ANY)] * m,
        out_specs=tuple(pl.BlockSpec(memory_space=pl.ANY) for _ in blocks),
        scratch_shapes=[
            pltpu.SemaphoreType.DMA((m, dp_size)),
            pltpu.SemaphoreType.DMA((m, dp_size)),
            pltpu.SemaphoreType.DMA((m,)),
        ],
        compiler_params=pltpu.CompilerParams(collective_id=0, has_side_effects=True),
    )(*blocks)


def contrast_kernel(
    scale_ref, shift_ref, own_slot_ref, slot_ref, raw_images_ref, feats_ref, gain_ref,
    upstream_out, image_out, images_ref,
):
    jb = pl.program_id(0)
    tc = feats_ref.shape[0]
    width = feats_ref.shape[1]
    rows = own_slot_ref.shape[0]
    scale = scale_ref[0]
    half_scale = 0.5 * scale
    half_shift = 0.5 * shift_ref[0]
    gain = gain_ref[...]

    feats = feats_ref[...].astype(jnp.float32)
    center = feats - jnp.sum(feats, axis=1, keepdims=True) / width
    spread = jnp.sum(center * center, axis=1, keepdims=True) / width
    inv_spread = lax.rsqrt(spread + 1e-05)
    normed = center * inv_spread * gain
    inv_norm = lax.rsqrt(jnp.sum(normed * normed, axis=1, keepdims=True) + 1e-06)
    captions = (normed * inv_norm).astype(jnp.bfloat16)
    places = jb * tc + lax.broadcasted_iota(jnp.int32, (tc, 1), 0)

    def weights_of(products, positive):
        half = 0.5 * jnp.tanh(half_scale * products + half_shift)
        return jnp.where(positive, half - 0.5, half + 0.5).astype(jnp.bfloat16)

    @pl.when(jb == 0)
    def _():
        def unit_chunk(c, carry):
            at = pl.ds(pl.multiple_of(c * tc, tc), tc)
            raw = raw_images_ref[at, :].astype(jnp.float32)
            images_ref[at, :] = (
                raw * lax.rsqrt(jnp.sum(raw * raw, axis=1, keepdims=True) + 1e-06)
            ).astype(images_ref.dtype)
            return carry

        lax.fori_loop(0, images_ref.shape[0] // tc, unit_chunk, 0)

    images = images_ref[...]
    products = lax.dot_general(
        captions, images, (((1,), (1,)), ((), ())), preferred_element_type=jnp.float32
    )
    weights = weights_of(products, slot_ref[...] == places)
    caption_grad = scale * jnp.dot(weights, images, preferred_element_type=jnp.float32)

    along = jnp.sum(caption_grad * normed, axis=1, keepdims=True)
    normed_grad = inv_norm * caption_grad - inv_norm * inv_norm * inv_norm * along * normed
    gained = gain * normed_grad
    spread_grad = -0.5 * inv_spread * inv_spread * inv_spread * jnp.sum(
        gained * center, axis=1, keepdims=True
    )
    center_grad = gained * inv_spread + (2.0 / width) * center * spread_grad
    feats_grad = center_grad - jnp.sum(center_grad, axis=1, keepdims=True) / width
    upstream_out[...] = feats_grad.astype(upstream_out.dtype)

    own_start = pl.multiple_of(lax.axis_index("dp") * rows, rows)
    own = images_ref[pl.ds(own_start, rows), :]
    own_scores = lax.dot_general(
        own, captions, (((1,), (1,)), ((), ())), preferred_element_type=jnp.float32
    )
    columns = jb * tc + lax.broadcasted_iota(jnp.int32, (1, tc), 1)
    own_weights = weights_of(own_scores, own_slot_ref[...] == columns)

    @pl.when(jb == 0)
    def _():
        image_out[...] = jnp.zeros_like(image_out)

    image_out[...] += scale * jnp.dot(own_weights, captions, preferred_element_type=jnp.float32)


def contrast_group(scale, shift, own_slot, slot_g, both_g, gain):
    group_rows, width = both_g.shape[0], gain.shape[0]
    rows = own_slot.shape[0]
    tc = 1024
    return pl.pallas_call(
        contrast_kernel,
        grid=(group_rows // tc,),
        out_shape=(
            jax.ShapeDtypeStruct((group_rows, width), jnp.bfloat16),
            jax.ShapeDtypeStruct((rows, width), jnp.float32),
        ),
        in_specs=[
            pl.BlockSpec(memory_space=pltpu.SMEM),
            pl.BlockSpec(memory_space=pltpu.SMEM),
            pl.BlockSpec((rows, 1), lambda j: (0, 0)),
            pl.BlockSpec((1, group_rows), lambda j: (0, 0)),
            pl.BlockSpec((group_rows, width), lambda j: (0, 0)),
            pl.BlockSpec((tc, width), lambda j: (j, 1)),
            pl.BlockSpec((1, width), lambda j: (0, 0)),
        ],
        out_specs=(
            pl.BlockSpec((tc, width), lambda j: (j, 0)),
            pl.BlockSpec((rows, width), lambda j: (0, 0)),
        ),
        scratch_shapes=[pltpu.VMEM((group_rows, width), jnp.bfloat16)],
        compiler_params=pltpu.CompilerParams(dimension_semantics=("arbitrary",)),
        cost_estimate=pl.CostEstimate(
            flops=4 * group_rows * (group_rows + rows) * width,
            bytes_accessed=3 * group_rows * width * 2 + rows * width * 4,
            transcendentals=group_rows * (group_rows + rows),
        ),
    )(
        scale,
        shift,
        own_slot.reshape((rows, 1)),
        slot_g.reshape((1, group_rows)),
        both_g,
        both_g,
        gain.reshape((1, width)),
    )


def unit_rows(values):
    return values * lax.rsqrt(jnp.sum(values * values, axis=1, keepdims=True) + 1e-06)


def text_embed(features, closing_layernorm_multiplier):
    center = features - jnp.mean(features, axis=1, keepdims=True)
    spread = jnp.mean(center * center, axis=1, keepdims=True)
    return unit_rows(center * lax.rsqrt(spread + 1e-05) * closing_layernorm_multiplier)


def sigmoid_weights(scores, labels):
    return (-labels * jax.nn.sigmoid(-labels * scores)).astype(jnp.bfloat16)


def shards(
    picture_embeds,
    matched_slot,
    summary_token_states,
    feedforward_inner_activations,
    closing_layernorm_multiplier,
    contracting_matrix,
    sharpness_factor,
    additive_shift_learned,
):
    similarity_multiplier = sharpness_factor[0]
    shift_value = additive_shift_learned[0]
    local_rows, width = picture_embeds.shape

    dp_size = lax.axis_size("dp")
    zero_size = lax.axis_size("zero")
    dp_place = lax.axis_index("dp")
    own_start = dp_place * local_rows
    transpose_route = [
        (a * zero_size + b, b * zero_size + a) for a in range(dp_size) for b in range(zero_size)
    ]

    ffa_cols = lax.all_to_all(
        feedforward_inner_activations, "dp", split_axis=1, concat_axis=0, tiled=True
    )
    weight_block = lax.ppermute(contracting_matrix, ("dp", "zero"), transpose_route)

    digits = jnp.zeros((16, local_rows), jnp.bfloat16)
    digits = digits.at[0].set((matched_slot // 256).astype(jnp.bfloat16))
    digits = digits.at[1].set((matched_slot % 256).astype(jnp.bfloat16))
    both = jnp.concatenate([picture_embeds, summary_token_states], axis=1)
    both_g, digits_g = gather_dp(both, digits)
    both_g = both_g.reshape((-1, both.shape[1]))
    ffa_cols, weight_block, both_g, digits_g = lax.optimization_barrier(
        (ffa_cols, weight_block, both_g, digits_g)
    )
    slot_g = (
        digits_g[:, 0, :].astype(jnp.int32) * 256 + digits_g[:, 1, :].astype(jnp.int32)
    ).reshape((-1,))
    unit_image, image_back = jax.vjp(unit_rows, picture_embeds.astype(jnp.float32))

    upstream_g, image_term = contrast_group(
        sharpness_factor,
        additive_shift_learned,
        matched_slot,
        slot_g,
        both_g,
        closing_layernorm_multiplier,
    )

    image_grad = image_back(image_term)[0]

    hidden_part = lax.dot_general(
        upstream_g,
        weight_block,
        (((1,), (1,)), ((), ())),
        preferred_element_type=jnp.float32,
    ).astype(jnp.bfloat16)
    hidden_grad = lax.all_to_all(hidden_part, "dp", split_axis=0, concat_axis=1, tiled=True)
    group_sum = lax.dot_general(
        ffa_cols, upstream_g, (((0,), (0,)), ((), ())), preferred_element_type=jnp.float32
    )
    down_parts = lax.all_to_all(group_sum, "zero", split_axis=1, concat_axis=0, tiled=True)
    down_block = jnp.sum(down_parts.reshape((zero_size,) + (group_sum.shape[0], -1)), axis=0)
    down_grad = lax.ppermute(down_block, ("dp", "zero"), transpose_route)
    return (image_grad, hidden_grad, down_grad)


def solution(mesh):
    placed = (
        P(("dp", "zero"), None),
        P(("dp", "zero")),
        P(("dp", "zero"), None),
        P(("dp", "zero"), None),
        P(),
        P("zero", None),
        P(),
        P(),
    )
    return jax.shard_map(
        shards,
        mesh=mesh,
        in_specs=placed,
        out_specs=(P(("dp", "zero"), None), P(("dp", "zero"), None), P("zero", "dp")),
        check_vma=False,
    )
```

```python
import functools

import jax
import jax.numpy as jnp
from jax import lax
from jax.experimental import pallas as pl
from jax.experimental.pallas import tpu as pltpu
from jax.sharding import PartitionSpec as P

MESH = pl.DeviceIdType.MESH


def gather_kernel(chips, m, *refs):
    block_refs, out_refs = refs[:m], refs[m : 2 * m]
    send_sem, recv_sem, local_sem = refs[2 * m :]
    me = lax.axis_index("dp")
    zz = lax.axis_index("zero")
    core = me % 2
    chip = me // 2
    sibling = me + 1 - 2 * core

    def peer(k):
        return ((chip + k) % chips) * 2 + core

    def source(k):
        return ((chip + chips - k) % chips) * 2 + core

    barrier = pltpu.get_barrier_semaphore()
    pl.semaphore_signal(barrier, inc=1, device_id=(sibling, zz), device_id_type=MESH)
    for k in range(1, chips):
        pl.semaphore_signal(barrier, inc=1, device_id=(peer(k), zz), device_id_type=MESH)
    pl.semaphore_wait(barrier, chips)

    def remote(i, src, slot, send_index, target):
        return pltpu.make_async_remote_copy(
            src_ref=src,
            dst_ref=out_refs[i].at[slot],
            send_sem=send_sem.at[i, send_index],
            recv_sem=recv_sem.at[i, slot],
            device_id=(target, zz),
            device_id_type=MESH,
        )

    locals_ = []
    sends = []
    for i in range(m):
        local = pltpu.make_async_copy(block_refs[i], out_refs[i].at[me], local_sem.at[i])
        local.start()
        locals_.append(local)
    for k in range(1, chips):
        for i in range(m):
            copy = remote(i, block_refs[i], me, k, peer(k))
            copy.start()
            sends.append(copy)
    for i in range(m):
        copy = remote(i, block_refs[i], me, 0, sibling)
        copy.start()
        sends.append(copy)
    for k in range(1, chips):
        s = source(k)
        for i in range(m):
            arrived = remote(i, out_refs[i].at[s], s, chips + k, sibling)
            arrived.wait_recv()
            arrived.start()
            sends.append(arrived)
    for k in range(chips):
        t = ((chip + k) % chips) * 2 + (1 - core)
        for i in range(m):
            remote(i, out_refs[i].at[t], t, 0, sibling).wait_recv()
    for copy in sends:
        copy.wait_send()
    for local in locals_:
        local.wait()


def gather_dp(*blocks):
    dp_size = lax.axis_size("dp")
    m = len(blocks)
    return pl.pallas_call(
        functools.partial(gather_kernel, dp_size // 2, m),
        out_shape=tuple(
            jax.ShapeDtypeStruct((dp_size,) + block.shape, block.dtype) for block in blocks
        ),
        in_specs=[pl.BlockSpec(memory_space=pl.ANY)] * m,
        out_specs=tuple(pl.BlockSpec(memory_space=pl.ANY) for _ in blocks),
        scratch_shapes=[
            pltpu.SemaphoreType.DMA((m, dp_size)),
            pltpu.SemaphoreType.DMA((m, dp_size)),
            pltpu.SemaphoreType.DMA((m,)),
        ],
        compiler_params=pltpu.CompilerParams(collective_id=0, has_side_effects=True),
    )(*blocks)


def contrast_kernel(
    scale_ref, shift_ref, own_slot_ref, slot_ref, raw_images_ref, feats_ref, gain_ref,
    upstream_out, image_out, images_ref,
):
    jb = pl.program_id(0)
    tc = feats_ref.shape[0]
    width = feats_ref.shape[1]
    rows = own_slot_ref.shape[0]
    scale = scale_ref[0]
    half_scale = 0.5 * scale
    half_shift = 0.5 * shift_ref[0]
    gain = gain_ref[...]

    feats = feats_ref[...].astype(jnp.float32)
    center = feats - jnp.sum(feats, axis=1, keepdims=True) / width
    spread = jnp.sum(center * center, axis=1, keepdims=True) / width
    inv_spread = lax.rsqrt(spread + 1e-05)
    normed = center * inv_spread * gain
    inv_norm = lax.rsqrt(jnp.sum(normed * normed, axis=1, keepdims=True) + 1e-06)
    captions = (normed * inv_norm).astype(jnp.bfloat16)
    places = jb * tc + lax.broadcasted_iota(jnp.int32, (tc, 1), 0)

    def weights_of(products, positive):
        half = 0.5 * jnp.tanh(half_scale * products + half_shift)
        return jnp.where(positive, half - 0.5, half + 0.5).astype(jnp.bfloat16)

    @pl.when(jb == 0)
    def _():
        def unit_chunk(c, carry):
            at = pl.ds(pl.multiple_of(c * tc, tc), tc)
            raw = raw_images_ref[at, :].astype(jnp.float32)
            images_ref[at, :] = (
                raw * lax.rsqrt(jnp.sum(raw * raw, axis=1, keepdims=True) + 1e-06)
            ).astype(images_ref.dtype)
            return carry

        lax.fori_loop(0, images_ref.shape[0] // tc, unit_chunk, 0)

    images = images_ref[...]
    products = lax.dot_general(
        captions, images, (((1,), (1,)), ((), ())), preferred_element_type=jnp.float32
    )
    weights = weights_of(products, slot_ref[...] == places)
    caption_grad = scale * jnp.dot(weights, images, preferred_element_type=jnp.float32)

    along = jnp.sum(caption_grad * normed, axis=1, keepdims=True)
    normed_grad = inv_norm * caption_grad - inv_norm * inv_norm * inv_norm * along * normed
    gained = gain * normed_grad
    spread_grad = -0.5 * inv_spread * inv_spread * inv_spread * jnp.sum(
        gained * center, axis=1, keepdims=True
    )
    center_grad = gained * inv_spread + (2.0 / width) * center * spread_grad
    feats_grad = center_grad - jnp.sum(center_grad, axis=1, keepdims=True) / width
    upstream_out[...] = feats_grad.astype(upstream_out.dtype)

    own_start = pl.multiple_of(lax.axis_index("dp") * rows, rows)
    own = images_ref[pl.ds(own_start, rows), :]
    own_scores = lax.dot_general(
        own, captions, (((1,), (1,)), ((), ())), preferred_element_type=jnp.float32
    )
    columns = jb * tc + lax.broadcasted_iota(jnp.int32, (1, tc), 1)
    own_weights = weights_of(own_scores, own_slot_ref[...] == columns)

    @pl.when(jb == 0)
    def _():
        image_out[...] = jnp.zeros_like(image_out)

    image_out[...] += scale * jnp.dot(own_weights, captions, preferred_element_type=jnp.float32)


def contrast_group(scale, shift, own_slot, slot_g, both_g, gain):
    group_rows, width = both_g.shape[0], gain.shape[0]
    rows = own_slot.shape[0]
    tc = 1024
    return pl.pallas_call(
        contrast_kernel,
        grid=(group_rows // tc,),
        out_shape=(
            jax.ShapeDtypeStruct((group_rows, width), jnp.bfloat16),
            jax.ShapeDtypeStruct((rows, width), jnp.float32),
        ),
        in_specs=[
            pl.BlockSpec(memory_space=pltpu.SMEM),
            pl.BlockSpec(memory_space=pltpu.SMEM),
            pl.BlockSpec((rows, 1), lambda j: (0, 0)),
            pl.BlockSpec((1, group_rows), lambda j: (0, 0)),
            pl.BlockSpec((group_rows, width), lambda j: (0, 0)),
            pl.BlockSpec((tc, width), lambda j: (j, 1)),
            pl.BlockSpec((1, width), lambda j: (0, 0)),
        ],
        out_specs=(
            pl.BlockSpec((tc, width), lambda j: (j, 0)),
            pl.BlockSpec((rows, width), lambda j: (0, 0)),
        ),
        scratch_shapes=[pltpu.VMEM((group_rows, width), jnp.bfloat16)],
        compiler_params=pltpu.CompilerParams(dimension_semantics=("arbitrary",)),
        cost_estimate=pl.CostEstimate(
            flops=4 * group_rows * (group_rows + rows) * width,
            bytes_accessed=3 * group_rows * width * 2 + rows * width * 4,
            transcendentals=group_rows * (group_rows + rows),
        ),
    )(
        scale,
        shift,
        own_slot.reshape((rows, 1)),
        slot_g.reshape((1, group_rows)),
        both_g,
        both_g,
        gain.reshape((1, width)),
    )


def unit_rows(values):
    return values * lax.rsqrt(jnp.sum(values * values, axis=1, keepdims=True) + 1e-06)


def text_embed(features, closing_layernorm_multiplier):
    center = features - jnp.mean(features, axis=1, keepdims=True)
    spread = jnp.mean(center * center, axis=1, keepdims=True)
    return unit_rows(center * lax.rsqrt(spread + 1e-05) * closing_layernorm_multiplier)


def sigmoid_weights(scores, labels):
    return (-labels * jax.nn.sigmoid(-labels * scores)).astype(jnp.bfloat16)


def shards(
    picture_embeds,
    matched_slot,
    summary_token_states,
    feedforward_inner_activations,
    closing_layernorm_multiplier,
    contracting_matrix,
    sharpness_factor,
    additive_shift_learned,
):
    similarity_multiplier = sharpness_factor[0]
    shift_value = additive_shift_learned[0]
    local_rows, width = picture_embeds.shape

    dp_size = lax.axis_size("dp")
    zero_size = lax.axis_size("zero")
    dp_place = lax.axis_index("dp")
    own_start = dp_place * local_rows
    transpose_route = [
        (a * zero_size + b, b * zero_size + a) for a in range(dp_size) for b in range(zero_size)
    ]

    ffa_cols = lax.all_to_all(
        feedforward_inner_activations, "dp", split_axis=1, concat_axis=0, tiled=True
    )
    digits = jnp.zeros((16, local_rows), jnp.bfloat16)
    digits = digits.at[0].set((matched_slot // 256).astype(jnp.bfloat16))
    digits = digits.at[1].set((matched_slot % 256).astype(jnp.bfloat16))
    both = jnp.concatenate([picture_embeds, summary_token_states], axis=1)
    both_g, digits_g = gather_dp(both, digits)
    both_g = both_g.reshape((-1, both.shape[1]))
    ffa_cols, weight_in, both_g, digits_g = lax.optimization_barrier(
        (ffa_cols, contracting_matrix, both_g, digits_g)
    )
    weight_block = lax.ppermute(weight_in, ("dp", "zero"), transpose_route)
    slot_g = (
        digits_g[:, 0, :].astype(jnp.int32) * 256 + digits_g[:, 1, :].astype(jnp.int32)
    ).reshape((-1,))
    unit_image, image_back = jax.vjp(unit_rows, picture_embeds.astype(jnp.float32))

    upstream_g, image_term = contrast_group(
        sharpness_factor,
        additive_shift_learned,
        matched_slot,
        slot_g,
        both_g,
        closing_layernorm_multiplier,
    )

    image_grad = image_back(image_term)[0]

    hidden_part = lax.dot_general(
        upstream_g,
        weight_block,
        (((1,), (1,)), ((), ())),
        preferred_element_type=jnp.float32,
    ).astype(jnp.bfloat16)
    hidden_grad = lax.all_to_all(hidden_part, "dp", split_axis=0, concat_axis=1, tiled=True)
    group_sum = lax.dot_general(
        ffa_cols, upstream_g, (((0,), (0,)), ((), ())), preferred_element_type=jnp.float32
    )
    down_parts = lax.all_to_all(group_sum, "zero", split_axis=1, concat_axis=0, tiled=True)
    down_block = jnp.sum(down_parts.reshape((zero_size,) + (group_sum.shape[0], -1)), axis=0)
    down_grad = lax.ppermute(down_block, ("dp", "zero"), transpose_route)
    return (image_grad, hidden_grad, down_grad)


def solution(mesh):
    placed = (
        P(("dp", "zero"), None),
        P(("dp", "zero")),
        P(("dp", "zero"), None),
        P(("dp", "zero"), None),
        P(),
        P("zero", None),
        P(),
        P(),
    )
    return jax.shard_map(
        shards,
        mesh=mesh,
        in_specs=placed,
        out_specs=(P(("dp", "zero"), None), P(("dp", "zero"), None), P("zero", "dp")),
        check_vma=False,
    )
```
